512 devices in a mesh: team: 16 (over y, core), cuts: 32 (over z, x).
Axes of the slice: x: 4, y: 8, z: 8, core: 2. Of those that a mesh axis runs over, the one named last changes fastest.
Arguments:
- position: float32 [3, 131072], P(None, ('team', 'cuts')), may hold values from -6 to 6
- velocity: float32 [3, 131072], P(None, ('team', 'cuts')), may hold values from -3 to 3
- accel_old: float32 [3, 131072], P(None, ('team', 'cuts')), may hold values from -6 to 6
- jerk_old: float32 [3, 131072], P(None, ('team', 'cuts')), may hold values from -16 to 16
- star_mass: float32 [131072], P(('team', 'cuts')), may hold values from 0.2 to 5
- active_index: int32 [16384], P(('team', 'cuts')), may hold values from 0 to 255, as said below
- active_count: int32 [512], P(('team', 'cuts')), may hold values from 1 to 32, 8192 in all
Outputs:
- corrected: float32 [12, 16384], P(None, ('team', 'cuts'))
The draws below stay inside these ranges and needn't reach their ends.
Inputs may be any that keep to these rules, and one draw needn't show every extreme that they name: `active_index`: each device's 32 entries are distinct. `active_count`: the counts of all devices sum to 8192.
All inputs are finite; a program needn't handle non-finite values.
Results may differ from the reference program's by a relative error of at most 0.00025.
Values sent between devices are 32-bit elements; how exact they have to be, the bound alone decides.
A program may use at most 64 MiB of HBM per device.

```python
import math
import jax
import jax.numpy as jnp
import numpy as np
from jax import lax

STARS_DEV = 256
ACT_DEV = 32
GROUPS = 512
STARS = 131072
ACTIVE = 8192


def draw_active_index(key, part):
    device_keys = jax.random.split(key, GROUPS)

    def choose(device_key):
        return jax.random.permutation(device_key, STARS_DEV)[:ACT_DEV]
    picks = jax.vmap(choose)(device_keys)
    return picks.reshape(-1).astype(jnp.int32)


def steps_of(stream_key, extent, shards, least, high):
    gain = 1.0
    for dim, blocks in shards:
        steps = jax.random.uniform(jax.random.fold_in(jax.random.fold_in(stream_key, 6), dim), (blocks,), jnp.float32, least / len(shards), high / len(shards))
        gain = gain * jnp.repeat(jnp.exp(steps), extent[dim] // blocks).reshape((-1,) + (1,) * (len(extent) - 1 - dim))
    return gain


def profile(amount, total, reach, skew):
    portions = [(1 << 20) // math.isqrt(rank ** skew) + 1 for rank in range(2, amount + 1)]
    rest, given = total - reach - (amount - 1), [1] * (amount - 1)
    while rest > 0:
        movable = [i for i in range(amount - 1) if given[i] < reach]
        whole, remaining = sum([portions[i] for i in movable]), rest
        for i in movable:
            more = min(reach - given[i], max(1, remaining * portions[i] // whole), rest)
            given[i] = given[i] + more
            rest = rest - more
    return np.array([reach] + given)


def ragged_sizes(stream_key, amount, total, limit, lean):
    if amount == 2:
        one = jax.random.randint(stream_key, (), max(1, total - limit), min(limit, total - 1) + 1)
        return jnp.stack([one, total - one])
    sizes = jnp.asarray(profile(amount, total, limit, lean), jnp.int32)
    twos = (amount - 1) // 2
    source_of, sink = sizes[1:1 + 2 * twos:2], sizes[2:2 + 2 * twos:2]
    slack = jnp.minimum(source_of - 1, limit - sink)
    passed = jax.random.randint(jax.random.fold_in(stream_key, 1), (twos,), 0, 1 << 20) % (slack + 1)
    sizes = sizes.at[1:1 + 2 * twos:2].set(source_of - passed).at[2:2 + 2 * twos:2].set(sink + passed)
    return sizes[jax.random.permutation(jax.random.fold_in(stream_key, 2), amount)]


def scatter_about(key, shape, deviation, limit, cuts=(), held_as=jnp.bfloat16):
    result = jax.random.normal(key, shape, jnp.float32) * deviation
    if len(cuts) > 0:
        result = steps_of(key, shape, cuts, -0.22, 0.18) * result
    return jnp.clip(result, min=-limit, max=limit).astype(held_as)


def setup_inputs(seed: int = 0) -> dict:
    splits = jax.random.split(jax.random.key(seed), 8)
    return {
        "position": scatter_about(splits[0], (3, STARS), 1.0, 6.0, ((1, 512),), jnp.float32),
        "velocity": scatter_about(splits[1], (3, STARS), 0.5, 3.0, ((1, 512),), jnp.float32),
        "accel_old": scatter_about(splits[2], (3, STARS), 1.0, 6.0, ((1, 512),), jnp.float32),
        "jerk_old": scatter_about(splits[3], (3, STARS), 3.0, 16.0, ((1, 512),), jnp.float32),
        "star_mass": jnp.clip(jnp.exp(math.log(5.0) - 3.218876 * jax.random.uniform(splits[4], (STARS,), jnp.float32) ** steps_of(splits[4], (STARS,), ((0, 512),), -0.2, 0.2)), 0.2, 5.0),
        "active_index": draw_active_index(jax.random.fold_in(splits[7], 71), 0),
        "active_count": ragged_sizes(splits[6], GROUPS, ACTIVE, ACT_DEV, 2).astype(jnp.int32),
    }


STEP_DT = 0.5
SOFTENING = 0.0004

def predict(position, velocity, accel_old, jerk_old):
    pred_pos = position + STEP_DT * (velocity + STEP_DT * (accel_old * 0.5 + STEP_DT * (jerk_old * (1.0 / 6.0))))
    pred_vel = velocity + STEP_DT * (accel_old + STEP_DT * (jerk_old * 0.5))
    return (pred_pos, pred_vel)

def pair_sums(sinks, field_pos, field_vel, weights):
    separation = [field_pos[component][:, None] - sinks[component][None, :] for component in range(3)]
    relative = [field_vel[component][:, None] - sinks[3 + component][None, :] for component in range(3)]
    radius_sq = separation[0] * separation[0] + separation[1] * separation[1] + separation[2] * separation[2] + SOFTENING
    inverse = lax.rsqrt(radius_sq)
    strength = weights[:, None] * (inverse * inverse * inverse)
    radial = 3.0 * (separation[0] * relative[0] + separation[1] * relative[1] + separation[2] * relative[2]) * (inverse * inverse)
    rows = [lax.optimization_barrier(jnp.sum(strength * separation[component], axis=0)) for component in range(3)]
    rows = rows + [lax.optimization_barrier(jnp.sum(strength * (relative[component] - radial * separation[component]), axis=0)) for component in range(3)]
    return jnp.stack(rows)

def slot_layout(counts, slot_count):
    groups = counts.shape[0]
    width = groups * slot_count
    within = jnp.arange(width, dtype=jnp.int32) % slot_count
    filled = jnp.broadcast_to(counts[:, None], (groups, slot_count)).reshape(-1)
    starts = jnp.cumsum(counts).astype(jnp.int32) - counts
    anchor = jnp.broadcast_to(starts[:, None], (groups, slot_count)).reshape(-1)
    return jnp.where(within < filled, anchor + within, width // 2).astype(jnp.int32)

def correct(sink_state, old_acc, old_jerk, new_rows, is_live):
    pred_pos = sink_state[:3]
    pred_vel = sink_state[3:]
    new_acc = new_rows[:3]
    new_jerk = new_rows[3:]
    change = old_acc - new_acc
    second = -6.0 * change - STEP_DT * (4.0 * old_jerk + 2.0 * new_jerk)
    third = 12.0 * change + 6.0 * STEP_DT * (old_jerk + new_jerk)
    new_pos = pred_pos + STEP_DT * STEP_DT * (second * (1.0 / 24.0) + third * (1.0 / 120.0))
    new_vel = pred_vel + STEP_DT * (second * (1.0 / 6.0) + third * (1.0 / 24.0))
    stacked = jnp.concatenate([new_pos, new_vel, new_acc, new_jerk], axis=0)
    return jnp.where(is_live[None, :], stacked, 0.0)

def reference(position, velocity, accel_old, jerk_old, star_mass, active_index, active_count):
    pred_pos, pred_vel = predict(position, velocity, accel_old, jerk_old)
    slots = active_index.shape[0]
    slot_count = slots // active_count.shape[0]
    owner = jnp.arange(slots, dtype=jnp.int32) // slot_count
    star_index = (owner * STARS_DEV + active_index).astype(jnp.int32)
    sink_state = jnp.concatenate([jnp.take(pred_pos, star_index, axis=1), jnp.take(pred_vel, star_index, axis=1)], axis=0)
    target = slot_layout(active_count, slot_count)
    packed = jnp.zeros((6, ACTIVE), jnp.float32).at[:, target].set(sink_state, mode='drop')
    weights = star_mass / STARS
    block_count = ACTIVE // 64
    blocked = packed.reshape(6, block_count, 64).transpose(1, 0, 2)

    def one_block(sinks):
        return pair_sums(sinks, pred_pos, pred_vel, weights)
    results = lax.map(one_block, blocked)
    forces = results.transpose(1, 0, 2).reshape(6, ACTIVE)
    new_rows = jnp.take(forces, jnp.minimum(target, ACTIVE - 1), axis=1)
    is_live = jnp.arange(slots, dtype=jnp.int32) % slot_count < jnp.take(active_count, owner)
    old_acc = jnp.take(accel_old, star_index, axis=1)
    old_jerk = jnp.take(jerk_old, star_index, axis=1)
    return correct(sink_state, old_acc, old_jerk, new_rows, is_live)
```

```python
import functools

import jax
import jax.numpy as jnp
from jax import lax
from jax.experimental import pallas as pl
from jax.experimental.pallas import tpu as pltpu
from jax.sharding import PartitionSpec as P

STEP_DT = 0.5
SOFTENING = 0.0004
MESH = pl.DeviceIdType.MESH
F32 = jnp.float32
BF16 = jnp.bfloat16
NT = (((1,), (1,)), ((), ()))


def split2(value):
    high = value.astype(BF16)
    return high, (value - high.astype(F32)).astype(BF16)


def split3(value):
    high = value.astype(BF16)
    rest = value - high.astype(F32)
    middle = rest.astype(BF16)
    return high, middle, (rest - middle.astype(F32)).astype(BF16)


def stack_pieces(rows, height):
    filled = sum(row.shape[0] for row in rows)
    rows = [row.astype(F32) for row in rows]
    rows = rows + [jnp.zeros((height - filled, rows[0].shape[1]), F32)]
    return jnp.concatenate(rows, axis=0).astype(BF16)


def predict(position, velocity, accel_old, jerk_old):
    pred_pos = position + STEP_DT * (
        velocity + STEP_DT * (accel_old * 0.5 + STEP_DT * (jerk_old * (1.0 / 6.0)))
    )
    pred_vel = velocity + STEP_DT * (accel_old + STEP_DT * (jerk_old * 0.5))
    return (pred_pos, pred_vel)


def correct(sink_state, old_acc, old_jerk, new_rows, is_live):
    pred_pos = sink_state[:3]
    pred_vel = sink_state[3:6]
    new_acc = new_rows[:3]
    new_jerk = new_rows[3:6]
    change = old_acc - new_acc
    second = -6.0 * change - STEP_DT * (4.0 * old_jerk + 2.0 * new_jerk)
    third = 12.0 * change + 6.0 * STEP_DT * (old_jerk + new_jerk)
    new_pos = pred_pos + STEP_DT * STEP_DT * (second * (1.0 / 24.0) + third * (1.0 / 120.0))
    new_vel = pred_vel + STEP_DT * (second * (1.0 / 6.0) + third * (1.0 / 24.0))
    stacked = jnp.concatenate([new_pos, new_vel, new_acc, new_jerk], axis=0)
    return jnp.where(is_live, stacked, 0.0)


def step_kernel(
    teams, cuts, xs, slots, stars,
    pos_ref, vel_ref, acc_ref, jerk_ref, mass_ref, index_ref, count_ref, out_ref,
    own_ref, star_ref, sink_ref, part_ref, sum_ref, weight_ref, wide_ref, lhs_ref, total_ref,
    star_send, star_recv, sink_send, sink_recv, part_send, part_recv,
):
    team = lax.axis_index("team")
    cut = lax.axis_index("cuts")
    zs = cuts // xs
    my_z = cut // xs
    my_x = lax.rem(cut, xs)
    chunk_devices = 2 * xs
    chunk = chunk_devices * slots
    tile = 16

    barrier = pltpu.get_barrier_semaphore()

    def greet_team(k, _):
        pl.semaphore_signal(
            barrier, inc=1, device_id=(lax.rem(team + k, teams), cut), device_id_type=MESH
        )
        return 0

    def greet_cuts(k, _):
        pl.semaphore_signal(
            barrier, inc=1, device_id=(team, lax.rem(cut + k, cuts)), device_id_type=MESH
        )
        return 0

    lax.fori_loop(1, teams, greet_team, 0)
    lax.fori_loop(1, cuts, greet_cuts, 0)

    acc_old = acc_ref[...]
    jerk_old = jerk_ref[...]
    pred_pos, pred_vel = predict(pos_ref[...], vel_ref[...], acc_old, jerk_old)
    weight = mass_ref[...] * (1.0 / (stars * teams * cuts))
    star_ref[team] = jnp.concatenate(
        [pred_pos, pred_vel, weight, jnp.zeros((1, stars), F32)], axis=0
    )
    picked = (
        lax.broadcasted_iota(jnp.int32, (stars, slots), 0) == index_ref[...]
    ).astype(F32).astype(BF16)
    source = jnp.concatenate([pred_pos, pred_vel, acc_old, jerk_old, jnp.zeros((4, stars), F32)], 0)
    pieces = split3(source)
    own = jnp.zeros((16, slots), F32)
    for piece in pieces:
        own = own + jnp.dot(piece, picked, preferred_element_type=F32)
    own_ref[...] = own
    sink_ref[cut] = jnp.concatenate([own[0:8], jnp.zeros((8, 128 - slots), F32)], axis=1)

    pl.semaphore_wait(barrier, teams + cuts - 2)

    def sink_copy(slot, device):
        return pltpu.make_async_remote_copy(
            src_ref=sink_ref.at[slot], dst_ref=sink_ref.at[slot],
            send_sem=sink_send.at[device], recv_sem=sink_recv.at[slot],
            device_id=(team, device), device_id_type=MESH,
        )

    def star_copy(slot, device):
        return pltpu.make_async_remote_copy(
            src_ref=star_ref.at[slot], dst_ref=star_ref.at[slot],
            send_sem=star_send.at[device], recv_sem=star_recv.at[slot],
            device_id=(device, cut), device_id_type=MESH,
        )

    def part_copy(source, slot, device):
        return pltpu.make_async_remote_copy(
            src_ref=part_ref.at[source], dst_ref=sum_ref.at[slot],
            send_sem=part_send.at[source], recv_sem=part_recv.at[slot],
            device_id=(team, device), device_id_type=MESH,
        )

    def send_star(k, _):
        star_copy(team, lax.rem(team + k, teams)).start()
        return 0

    def send_sink(k, _):
        sink_copy(cut, lax.rem(cut + k, cuts)).start()
        return 0

    lax.fori_loop(1, teams, send_star, 0)
    lax.fori_loop(1, cuts, send_sink, 0)

    def star_weights(block):
        state = star_ref[block]
        mass = state[6:7]
        mass_pos = mass * state[0:3]
        mass_vel = mass * state[3:6]
        empty3 = jnp.zeros((3, stars), F32)
        empty9 = jnp.zeros((9, stars), F32)
        plain = stack_pieces([*split3(mass_pos), *split3(mass_vel), *split3(mass), empty3], 32)
        cross = stack_pieces([empty9, *split3(-3.0 * mass_pos), empty3, *split3(3.0 * mass)], 32)
        weight_ref[block] = jnp.concatenate([plain, plain, cross, cross], axis=1)

    def take_star(k, _):
        block = lax.rem(team + k, teams)
        star_copy(block, block).wait_recv()
        star_weights(block)
        return 0

    star_weights(team)
    lax.fori_loop(1, teams, take_star, 0)

    def take_sink(k, _):
        block = lax.rem(cut + k, cuts)
        sink_copy(block, block).wait_recv()
        return 0

    lax.fori_loop(1, cuts, take_sink, 0)

    def fill(block, buffer):
        state = star_ref[block]
        for step in range(chunk // tile):
            rows = slice(step * tile, (step + 1) * tile)
            sinks = [wide_ref[c, rows, :] for c in range(6)]
            sinks = [jnp.concatenate([value] * (stars // 128), axis=1) for value in sinks]
            sep = [state[c : c + 1] - sinks[c] for c in range(3)]
            rel = [state[3 + c : 4 + c] - sinks[3 + c] for c in range(3)]
            radius_sq = sep[0] * sep[0] + (sep[1] * sep[1] + (sep[2] * sep[2] + SOFTENING))
            radial = sep[0] * rel[0] + sep[1] * rel[1] + sep[2] * rel[2]
            inverse = lax.rsqrt(radius_sq)
            inverse_sq = inverse * inverse
            cube = inverse_sq * inverse
            fifth = (cube * inverse_sq) * radial
            for part, value in enumerate((*split2(cube), *split2(fifth))):
                lhs_ref[buffer, rows, part * stars : (part + 1) * stars] = value

    def add(block, buffer):
        total_ref[...] += lax.dot_general(
            lhs_ref[buffer], weight_ref[block], NT, preferred_element_type=F32
        )

    def one_chunk(g, _):
        devices = []
        for side in range(2):
            z = lax.rem(my_z + (zs // 2 - 1 - g if side == 0 else zs // 2 + g), zs)
            for j in range(xs):
                devices.append(z * xs + lax.rem(my_x + j, xs))
        states = []
        for i, device in enumerate(devices):
            state = sink_ref[device]
            states.append(state[:, :slots])
            columns = jnp.transpose(state)[:slots, :]
            for c in range(6):
                wide_ref[c, i * slots : (i + 1) * slots, :] = jnp.broadcast_to(
                    columns[:, c : c + 1], (slots, 128)
                )
        total_ref[...] = jnp.zeros_like(total_ref)
        fill(0, 0)

        def two_blocks(k, _):
            block = 2 * k
            fill(block + 1, 1)
            add(block, 0)
            fill(jnp.minimum(block + 2, teams - 1), 0)
            add(block + 1, 1)
            return 0

        lax.fori_loop(0, teams // 2, two_blocks, 0)
        sums = jnp.concatenate([total_ref[...], jnp.zeros((chunk, 96), F32)], axis=1)
        for i, device in enumerate(devices):
            rows = jnp.transpose(
                jnp.concatenate([sums[i * slots : (i + 1) * slots], jnp.zeros((128 - slots, 128), F32)], 0)
            )
            state = sink_ref[device]
            pos = state[0:3]
            vel = state[3:6]
            whole = rows[18:19] + rows[19:20] + rows[20:21]
            cross = rows[21:22] + rows[22:23] + rows[23:24]
            new_acc = (rows[0:3] + rows[3:6] + rows[6:9]) - pos * whole
            new_jerk = (rows[9:12] + rows[12:15] + rows[15:18]) - vel * whole + pos * cross
            result = jnp.concatenate([new_acc, new_jerk, jnp.zeros((2, 128), F32)], axis=0)
            if i == 0:
                mine = g == zs // 2 - 1

                @pl.when(mine)
                def _():
                    sum_ref[cut] = result

                @pl.when(jnp.logical_not(mine))
                def _():
                    part_ref[device] = result
                    part_copy(device, cut, device).start()
            else:
                part_ref[device] = result
                part_copy(device, cut, device).start()
        return 0

    lax.fori_loop(0, zs // 2, one_chunk, 0)

    def take_part(k, total):
        block = lax.rem(cut + k, cuts)
        part_copy(block, block, block).wait_recv()
        return total + sum_ref[block]

    total = lax.fori_loop(1, cuts, take_part, sum_ref[cut])
    own_rows = own_ref[...]
    is_live = lax.broadcasted_iota(jnp.int32, (1, slots), 1) < count_ref[...]
    out_ref[...] = correct(
        own_rows[0:6], own_rows[6:9], own_rows[9:12], total[:, :slots], is_live
    )

    def end_star(k, _):
        device = lax.rem(team + k, teams)
        star_copy(team, device).wait_send()
        return 0

    def end_sink(k, _):
        device = lax.rem(cut + k, cuts)
        sink_copy(cut, device).wait_send()
        part_copy(device, cut, device).wait_send()
        return 0

    lax.fori_loop(1, teams, end_star, 0)
    lax.fori_loop(1, cuts, end_sink, 0)


def solution(mesh):
    teams = mesh.shape["team"]
    cuts = mesh.shape["cuts"]
    xs = 4

    def local(position, velocity, accel_old, jerk_old, star_mass, active_index, active_count):
        stars = position.shape[1]
        slots = active_index.shape[0]
        chunk = 2 * xs * slots
        vmem = pl.BlockSpec(memory_space=pltpu.VMEM)
        dma = pltpu.SemaphoreType.DMA
        return pl.pallas_call(
            functools.partial(step_kernel, teams, cuts, xs, slots, stars),
            out_shape=jax.ShapeDtypeStruct((12, slots), F32),
            in_specs=[vmem] * 7,
            out_specs=vmem,
            scratch_shapes=[
                pltpu.VMEM((16, slots), F32),
                pltpu.VMEM((teams, 8, stars), F32),
                pltpu.VMEM((cuts, 8, 128), F32),
                pltpu.VMEM((cuts, 8, 128), F32),
                pltpu.VMEM((cuts, 8, 128), F32),
                pltpu.VMEM((teams, 32, 4 * stars), BF16),
                pltpu.VMEM((6, chunk, 128), F32),
                pltpu.VMEM((2, chunk, 4 * stars), BF16),
                pltpu.VMEM((chunk, 32), F32),
                dma((teams,)), dma((teams,)), dma((cuts,)), dma((cuts,)), dma((cuts,)), dma((cuts,)),
            ],
            compiler_params=pltpu.CompilerParams(collective_id=0, has_side_effects=True),
            name="hermite_step",
        )(
            position, velocity, accel_old, jerk_old,
            star_mass.reshape(1, stars), active_index.reshape(1, slots), active_count.reshape(1, 1),
        )

    column = P(None, ("team", "cuts"))
    line = P(("team", "cuts"))
    return jax.shard_map(
        local, mesh=mesh, in_specs=(column, column, column, column, line, line, line),
        out_specs=column, check_vma=False,
    )
```

```python
import functools

import jax
import jax.numpy as jnp
from jax import lax
from jax.experimental import pallas as pl
from jax.experimental.pallas import tpu as pltpu
from jax.sharding import PartitionSpec as P

STEP_DT = 0.5
SOFTENING = 0.0004
MESH = pl.DeviceIdType.MESH
F32 = jnp.float32
BF16 = jnp.bfloat16


def split2(value):
    high = value.astype(BF16)
    return high, (value - high.astype(F32)).astype(BF16)


def split3(value):
    high = value.astype(BF16)
    rest = value - high.astype(F32)
    middle = rest.astype(BF16)
    return high, middle, (rest - middle.astype(F32)).astype(BF16)


def stack_pieces(rows, height):
    filled = sum(row.shape[0] for row in rows)
    rows = [row.astype(F32) for row in rows]
    rows = rows + [jnp.zeros((height - filled, rows[0].shape[1]), F32)]
    return jnp.concatenate(rows, axis=0).astype(BF16)


def predict(position, velocity, accel_old, jerk_old):
    pred_pos = position + STEP_DT * (
        velocity + STEP_DT * (accel_old * 0.5 + STEP_DT * (jerk_old * (1.0 / 6.0)))
    )
    pred_vel = velocity + STEP_DT * (accel_old + STEP_DT * (jerk_old * 0.5))
    return (pred_pos, pred_vel)


def correct(sink_state, old_acc, old_jerk, new_rows, is_live):
    pred_pos = sink_state[:3]
    pred_vel = sink_state[3:6]
    new_acc = new_rows[:3]
    new_jerk = new_rows[3:6]
    change = old_acc - new_acc
    second = -6.0 * change - STEP_DT * (4.0 * old_jerk + 2.0 * new_jerk)
    third = 12.0 * change + 6.0 * STEP_DT * (old_jerk + new_jerk)
    new_pos = pred_pos + STEP_DT * STEP_DT * (second * (1.0 / 24.0) + third * (1.0 / 120.0))
    new_vel = pred_vel + STEP_DT * (second * (1.0 / 6.0) + third * (1.0 / 24.0))
    stacked = jnp.concatenate([new_pos, new_vel, new_acc, new_jerk], axis=0)
    return jnp.where(is_live, stacked, 0.0)


def step_kernel(
    teams, cuts, xs, slots, stars, cores,
    pos_ref, vel_ref, acc_ref, jerk_ref, mass_ref, index_ref, count_ref, out_ref,
    own_ref, star_ref, sink_ref, part_ref, sum_ref, plain_ref, cross_ref, wide_ref,
    star_send, star_recv, sink_send, sink_recv, part_send, part_recv,
):
    team = lax.axis_index("team")
    cut = lax.axis_index("cuts")
    zs = cuts // xs
    ys = teams // cores
    my_z = cut // xs
    my_x = lax.rem(cut, xs)
    my_y = team // cores
    my_core = lax.rem(team, cores)
    group = xs * slots
    tile = 16
    tiles = 2 * group // tile

    barrier = pltpu.get_barrier_semaphore()

    def greet_team(k, _):
        pl.semaphore_signal(
            barrier, inc=1, device_id=(lax.rem(team + k, teams), cut), device_id_type=MESH
        )
        return 0

    def greet_cuts(k, _):
        pl.semaphore_signal(
            barrier, inc=1, device_id=(team, lax.rem(cut + k, cuts)), device_id_type=MESH
        )
        return 0

    lax.fori_loop(1, teams, greet_team, 0)
    lax.fori_loop(1, cuts, greet_cuts, 0)

    acc_old = acc_ref[...]
    jerk_old = jerk_ref[...]
    pred_pos, pred_vel = predict(pos_ref[...], vel_ref[...], acc_old, jerk_old)
    weight = mass_ref[...] * (1.0 / (stars * teams * cuts))
    star_ref[team] = jnp.concatenate(
        [pred_pos, pred_vel, weight, jnp.zeros((1, stars), F32)], axis=0
    )
    index = jnp.concatenate(
        [index_ref[...], jnp.full((1, 256 - slots), -1, jnp.int32)], axis=1
    )
    picked = (
        lax.broadcasted_iota(jnp.int32, (stars, 256), 0) == index
    ).astype(F32).astype(BF16)
    source = jnp.concatenate([pred_pos, pred_vel, acc_old, jerk_old, jnp.zeros((4, stars), F32)], 0)

    def pick(pick_acc):
        pltpu.matmul_push_rhs(picked, staging_register=0, mxu_index=0)
        for n, piece in enumerate(split3(source)):
            pltpu.matmul_acc_lhs(pick_acc, piece, load_staged_rhs=0 if n == 0 else None)
        own_ref[...] = pltpu.matmul_pop(pick_acc)[:, :slots]

    pl.run_scoped(pick, pltpu.ACC(0)((16, 256), F32))
    own = own_ref[...]
    lane_x = lax.broadcasted_iota(jnp.int32, (8, group), 1) // slots
    state = jnp.concatenate([own[0:6], jnp.zeros((2, slots), F32)], axis=0)
    sink_ref[cut] = jnp.where(lane_x == my_x, jnp.concatenate([state] * xs, axis=1), 0.0)

    def star_weights(block):
        state = star_ref[block]
        mass = state[6:7]
        mass_pos = mass * state[0:3]
        mass_vel = mass * state[3:6]
        empty3 = jnp.zeros((3, stars), F32)
        empty9 = jnp.zeros((9, stars), F32)
        plain_ref[block, :32, :] = stack_pieces(
            [*split3(mass_pos), *split3(mass_vel), *split3(mass), empty3], 32
        )
        cross_ref[block, :32, :] = stack_pieces(
            [empty9, *split3(-3.0 * mass_pos), empty3, *split3(3.0 * mass)], 32
        )

    plain_ref[...] = jnp.zeros_like(plain_ref)
    cross_ref[...] = jnp.zeros_like(cross_ref)
    star_weights(team)

    pl.semaphore_wait(barrier, teams + cuts - 2)

    def sink_copy(slot, device):
        return pltpu.make_async_remote_copy(
            src_ref=sink_ref.at[slot], dst_ref=sink_ref.at[slot],
            send_sem=sink_send.at[device], recv_sem=sink_recv.at[slot],
            device_id=(team, device), device_id_type=MESH,
        )

    def star_copy(slot, device):
        return pltpu.make_async_remote_copy(
            src_ref=star_ref.at[slot], dst_ref=star_ref.at[slot],
            send_sem=star_send.at[device], recv_sem=star_recv.at[slot],
            device_id=(device, cut), device_id_type=MESH,
        )

    def part_copy(z, slot, device):
        return pltpu.make_async_remote_copy(
            src_ref=part_ref.at[z], dst_ref=sum_ref.at[slot],
            send_sem=part_send.at[device], recv_sem=part_recv.at[slot],
            device_id=(team, device), device_id_type=MESH,
        )

    def nth_block(k):
        step = k // cores
        y = (step + 1) // 2 * (2 * lax.rem(step, 2) - 1)
        y = lax.rem(my_y + y + ys, ys)
        return y * cores + lax.rem(my_core + k, cores)

    def send_star(k, _):
        star_copy(team, nth_block(k)).start()
        return 0

    def send_sink(k, _):
        sink_copy(cut, lax.rem(cut + k, cuts)).start()
        return 0

    lax.fori_loop(1, cuts, send_sink, 0)
    lax.fori_loop(1, teams, send_star, 0)

    def devices_of(offset):
        z = lax.rem(my_z + offset, zs)
        return z, [z * xs + lax.rem(my_x + j, xs) for j in range(xs)]

    def open_chunk(offsets, first):
        states = []
        for side, offset in enumerate(offsets):
            _, devices = devices_of(offset)
            for device in devices[1:] if first and side == 0 else devices:
                sink_copy(device, device).wait_recv()
            state = sink_ref[devices[0]]
            for device in devices[1:]:
                state = state + sink_ref[device]
            columns = jnp.transpose(state)
            for c in range(6):
                wide_ref[c, side * group : (side + 1) * group, :] = jnp.broadcast_to(
                    columns[:, c : c + 1], (group, 128)
                )
            states.append(state)
        return states

    def pairs(block, plain_acc, cross_acc):
        pltpu.matmul_push_rhs(plain_ref[block], staging_register=0, mxu_index=0, transpose=True)
        pltpu.matmul_push_rhs(cross_ref[block], staging_register=0, mxu_index=1, transpose=True)
        state = star_ref[block]
        for step in range(tiles):
            rows = slice(step * tile, (step + 1) * tile)
            sinks = [wide_ref[c, rows, :] for c in range(6)]
            sinks = [jnp.concatenate([value] * (stars // 128), axis=1) for value in sinks]
            sep = [state[c : c + 1] - sinks[c] for c in range(3)]
            rel = [state[3 + c : 4 + c] - sinks[3 + c] for c in range(3)]
            radius_sq = sep[0] * sep[0] + (sep[1] * sep[1] + (sep[2] * sep[2] + SOFTENING))
            radial = sep[0] * rel[0] + sep[1] * rel[1] + sep[2] * rel[2]
            inverse = lax.rsqrt(radius_sq)
            inverse_sq = inverse * inverse
            cube = inverse_sq * inverse
            fifth = (cube * inverse_sq) * radial
            load = 0 if step == 0 else None
            high, low = split2(cube)
            pltpu.matmul_acc_lhs(plain_acc[step], high, load_staged_rhs=load)
            pltpu.matmul_acc_lhs(plain_acc[step], low)
            high, low = split2(fifth)
            pltpu.matmul_acc_lhs(cross_acc[step], high, load_staged_rhs=load)
            pltpu.matmul_acc_lhs(cross_acc[step], low)

    def close_chunk(offsets, first, plain_acc, cross_acc):
        half = tiles // 2
        for side, offset in enumerate(offsets):
            sums = [
                (pltpu.matmul_pop(plain_acc[t]) + pltpu.matmul_pop(cross_acc[t]))[:, :128]
                for t in range(side * half, (side + 1) * half)
            ]
            rows = jnp.transpose(jnp.concatenate(sums, axis=0))
            z, devices = devices_of(offset)
            state = sink_ref[devices[0]]
            for device in devices[1:]:
                state = state + sink_ref[device]
            pos = state[0:3]
            vel = state[3:6]
            whole = rows[18:19] + rows[19:20] + rows[20:21]
            cross = rows[21:22] + rows[22:23] + rows[23:24]
            new_acc = (rows[0:3] + rows[3:6] + rows[6:9]) - pos * whole
            new_jerk = (rows[9:12] + rows[12:15] + rows[15:18]) - vel * whole + pos * cross
            result = jnp.concatenate([new_acc, new_jerk, jnp.zeros((2, group), F32)], axis=0)
            part_ref[z] = result
            if first and side == 0:
                sum_ref[cut] = result
                devices = devices[1:]
            for device in devices:
                part_copy(z, cut, device).start()

    def compute(*accumulators):
        plain_acc = accumulators[:tiles]
        cross_acc = accumulators[tiles:]

        open_chunk((0, 1), True)

        def near_block(k, _):
            block = nth_block(k)

            @pl.when(k > 0)
            def _():
                star_copy(block, block).wait_recv()
                star_weights(block)

            pairs(block, plain_acc, cross_acc)
            return 0

        lax.fori_loop(0, teams, near_block, 0)
        close_chunk((0, 1), True, plain_acc, cross_acc)

        def one_chunk(g, _):
            offsets = (zs // 2 + 1 - g, zs // 2 + g)
            open_chunk(offsets, False)

            def next_block(k, _):
                pairs(k, plain_acc, cross_acc)
                return 0

            lax.fori_loop(0, teams, next_block, 0)
            close_chunk(offsets, False, plain_acc, cross_acc)
            return 0

        lax.fori_loop(1, zs // 2, one_chunk, 0)

    pl.run_scoped(
        compute,
        *[pltpu.ACC(0)((tile, 256), F32) for _ in range(tiles)],
        *[pltpu.ACC(1)((tile, 256), F32) for _ in range(tiles)],
    )

    def take_part(k, total):
        block = lax.rem(cut + k, cuts)
        part_copy(0, block, block).wait_recv()
        return total + sum_ref[block]

    total = lax.fori_loop(1, cuts, take_part, sum_ref[cut])
    total = jnp.where(lane_x == my_x, total, 0.0)
    rows = total[:, :slots]
    for x in range(1, xs):
        rows = rows + total[:, x * slots : (x + 1) * slots]
    own_rows = own_ref[...]
    is_live = lax.broadcasted_iota(jnp.int32, (1, slots), 1) < count_ref[...]
    out_ref[...] = correct(own_rows[0:6], own_rows[6:9], own_rows[9:12], rows, is_live)

    def end_star(k, _):
        star_copy(team, lax.rem(team + k, teams)).wait_send()
        return 0

    def end_sink(k, _):
        device = lax.rem(cut + k, cuts)
        sink_copy(cut, device).wait_send()
        part_copy(0, cut, device).wait_send()
        return 0

    lax.fori_loop(1, teams, end_star, 0)
    lax.fori_loop(1, cuts, end_sink, 0)


def solution(mesh):
    teams = mesh.shape["team"]
    cuts = mesh.shape["cuts"]
    xs = 4
    cores = 2

    def local(position, velocity, accel_old, jerk_old, star_mass, active_index, active_count):
        stars = position.shape[1]
        slots = active_index.shape[0]
        group = xs * slots
        vmem = pl.BlockSpec(memory_space=pltpu.VMEM)
        dma = pltpu.SemaphoreType.DMA
        return pl.pallas_call(
            functools.partial(step_kernel, teams, cuts, xs, slots, stars, cores),
            out_shape=jax.ShapeDtypeStruct((12, slots), F32),
            in_specs=[vmem] * 7,
            out_specs=vmem,
            scratch_shapes=[
                pltpu.VMEM((16, slots), F32),
                pltpu.VMEM((teams, 8, stars), F32),
                pltpu.VMEM((cuts, 8, group), F32),
                pltpu.VMEM((cuts // xs, 8, group), F32),
                pltpu.VMEM((cuts, 8, group), F32),
                pltpu.VMEM((teams, 256, stars), BF16),
                pltpu.VMEM((teams, 256, stars), BF16),
                pltpu.VMEM((6, 2 * group, 128), F32),
                dma((teams,)), dma((teams,)), dma((cuts,)), dma((cuts,)), dma((cuts,)), dma((cuts,)),
            ],
            compiler_params=pltpu.CompilerParams(collective_id=0, has_side_effects=True),
            name="hermite_step",
        )(
            position, velocity, accel_old, jerk_old,
            star_mass.reshape(1, stars), active_index.reshape(1, slots), active_count.reshape(1, 1),
        )

    column = P(None, ("team", "cuts"))
    line = P(("team", "cuts"))
    return jax.shard_map(
        local, mesh=mesh, in_specs=(column, column, column, column, line, line, line),
        out_specs=column, check_vma=False,
    )
```

```python
import functools

import jax
import jax.numpy as jnp
from jax import lax
from jax.experimental import pallas as pl
from jax.experimental.pallas import tpu as pltpu
from jax.sharding import PartitionSpec as P

STEP_DT = 0.5
SOFTENING = 0.0004
MESH = pl.DeviceIdType.MESH
F32 = jnp.float32
BF16 = jnp.bfloat16


def split2(value):
    high = value.astype(BF16)
    return high, (value - high.astype(F32)).astype(BF16)


def split3(value):
    high = value.astype(BF16)
    rest = value - high.astype(F32)
    middle = rest.astype(BF16)
    return high, middle, (rest - middle.astype(F32)).astype(BF16)


def stack_pieces(rows, height):
    filled = sum(row.shape[0] for row in rows)
    rows = [row.astype(F32) for row in rows]
    rows = rows + [jnp.zeros((height - filled, rows[0].shape[1]), F32)]
    return jnp.concatenate(rows, axis=0).astype(BF16)


def predict(position, velocity, accel_old, jerk_old):
    pred_pos = position + STEP_DT * (
        velocity + STEP_DT * (accel_old * 0.5 + STEP_DT * (jerk_old * (1.0 / 6.0)))
    )
    pred_vel = velocity + STEP_DT * (accel_old + STEP_DT * (jerk_old * 0.5))
    return (pred_pos, pred_vel)


def correct(sink_state, old_acc, old_jerk, new_rows, is_live):
    pred_pos = sink_state[:3]
    pred_vel = sink_state[3:6]
    new_acc = new_rows[:3]
    new_jerk = new_rows[3:6]
    change = old_acc - new_acc
    second = -6.0 * change - STEP_DT * (4.0 * old_jerk + 2.0 * new_jerk)
    third = 12.0 * change + 6.0 * STEP_DT * (old_jerk + new_jerk)
    new_pos = pred_pos + STEP_DT * STEP_DT * (second * (1.0 / 24.0) + third * (1.0 / 120.0))
    new_vel = pred_vel + STEP_DT * (second * (1.0 / 6.0) + third * (1.0 / 24.0))
    stacked = jnp.concatenate([new_pos, new_vel, new_acc, new_jerk], axis=0)
    return jnp.where(is_live, stacked, 0.0)


def near_first(ys, zs):
    spans = [range(-((n - 1) // 2), n // 2 + 1) for n in (ys, zs)]
    return sorted(
        ((dy, dz) for dy in spans[0] for dz in spans[1]),
        key=lambda offset: (abs(offset[0]) + abs(offset[1]), abs(offset[0])),
    )


def looked_up(table, base, index):
    per_word = 1
    while base ** (per_word + 1) < 2**31:
        per_word += 1
    word_index = index // per_word
    place = lax.rem(index, per_word)
    word = jnp.int32(0)
    for n in range(-(-len(table) // per_word)):
        digits = table[n * per_word : (n + 1) * per_word]
        value = sum(digit * base**r for r, digit in enumerate(digits))
        word = jnp.where(word_index == n, jnp.int32(value), word)
    result = jnp.int32(0)
    for r in range(per_word):
        result = jnp.where(place == r, lax.rem(word // base**r, base), result)
    return result


def step_kernel(
    teams, cuts, xs, slots, stars, cores,
    pos_ref, vel_ref, acc_ref, jerk_ref, mass_ref, index_ref, count_ref, out_ref,
    own_ref, star_ref, sink_ref, part_ref, sum_ref, plain_ref, cross_ref, wide_ref,
    star_send, star_recv, sink_send, sink_recv, part_send, part_recv,
):
    team = lax.axis_index("team")
    cut = lax.axis_index("cuts")
    zs = cuts // xs
    ys = teams // cores
    my_z = cut // xs
    my_x = lax.rem(cut, xs)
    my_y = team // cores
    my_core = lax.rem(team, cores)
    group = xs * slots
    peers = cores * xs
    blocks = ys * zs
    tile = 16
    half_tiles = group // tile
    tiles = cores * half_tiles
    me = my_core * xs + my_x
    order = near_first(ys, zs)
    low_y, high_y = min(o[0] for o in order), max(o[0] for o in order)
    low_z, high_z = min(o[1] for o in order), max(o[1] for o in order)
    table = [(dy - low_y) * zs + (dz - low_z) for dy, dz in order]

    def peer_id(k):
        peer = lax.rem(me + k, peers)
        return (my_y * cores + peer // xs, my_z * xs + lax.rem(peer, xs))

    def side_id(dy, dz):
        y = lax.rem(my_y + dy + ys, ys)
        z = lax.rem(my_z + dz + zs, zs)
        return (y * cores + my_core, z * xs + my_x)

    sides = ((-1, 0), (1, 0), (0, -1), (0, 1))
    barrier = pltpu.get_barrier_semaphore()
    for dy, dz in sides:
        pl.semaphore_signal(barrier, inc=1, device_id=side_id(dy, dz), device_id_type=MESH)
    for k in range(1, peers):
        pl.semaphore_signal(barrier, inc=1, device_id=peer_id(k), device_id_type=MESH)

    acc_old = acc_ref[...]
    jerk_old = jerk_ref[...]
    pred_pos, pred_vel = predict(pos_ref[...], vel_ref[...], acc_old, jerk_old)
    weight = mass_ref[...] * (1.0 / (stars * teams * cuts))
    home = my_y * zs + my_z
    star_ref[home] = jnp.concatenate(
        [pred_pos, pred_vel, weight, jnp.zeros((1, stars), F32)], axis=0
    )
    index = jnp.concatenate(
        [index_ref[...], jnp.full((1, 256 - slots), -1, jnp.int32)], axis=1
    )
    picked = (
        lax.broadcasted_iota(jnp.int32, (stars, 256), 0) == index
    ).astype(F32).astype(BF16)
    source = jnp.concatenate([pred_pos, pred_vel, acc_old, jerk_old, jnp.zeros((4, stars), F32)], 0)

    def pick(pick_acc):
        pltpu.matmul_push_rhs(picked, staging_register=0, mxu_index=0)
        for n, piece in enumerate(split3(source)):
            pltpu.matmul_acc_lhs(pick_acc, piece, load_staged_rhs=0 if n == 0 else None)
        own_ref[...] = pltpu.matmul_pop(pick_acc)[:, :slots]

    pl.run_scoped(pick, pltpu.ACC(0)((16, 256), F32))
    own = own_ref[...]
    lane_x = lax.broadcasted_iota(jnp.int32, (8, group), 1) // slots
    state = jnp.concatenate([own[0:6], jnp.zeros((2, slots), F32)], axis=0)
    sink_ref[me] = jnp.where(lane_x == my_x, jnp.concatenate([state] * xs, axis=1), 0.0)

    def star_weights(block, buffer):
        state = star_ref[block]
        mass = state[6:7]
        mass_pos = mass * state[0:3]
        mass_vel = mass * state[3:6]
        empty3 = jnp.zeros((3, stars), F32)
        empty9 = jnp.zeros((9, stars), F32)
        plain_ref[buffer, :32, :] = stack_pieces(
            [*split3(mass_pos), *split3(mass_vel), *split3(mass), empty3], 32
        )
        cross_ref[buffer, :32, :] = stack_pieces(
            [empty9, *split3(-3.0 * mass_pos), empty3, *split3(3.0 * mass)], 32
        )

    plain_ref[...] = jnp.zeros_like(plain_ref)
    cross_ref[...] = jnp.zeros_like(cross_ref)
    star_weights(home, 0)

    pl.semaphore_wait(barrier, len(sides) + peers - 1)

    def sink_copy(k):
        return pltpu.make_async_remote_copy(
            src_ref=sink_ref.at[me], dst_ref=sink_ref.at[me],
            send_sem=sink_send, recv_sem=sink_recv,
            device_id=peer_id(k), device_id_type=MESH,
        )

    def part_copy(k):
        return pltpu.make_async_remote_copy(
            src_ref=part_ref.at[lax.rem(me + k, peers) // xs], dst_ref=sum_ref.at[me],
            send_sem=part_send, recv_sem=part_recv,
            device_id=peer_id(k), device_id_type=MESH,
        )

    def star_copy(block, side):
        return pltpu.make_async_remote_copy(
            src_ref=star_ref.at[block], dst_ref=star_ref.at[block],
            send_sem=star_send.at[side], recv_sem=star_recv.at[block],
            device_id=side_id(*sides[side]), device_id_type=MESH,
        )

    def all_but_me(ref, send_sem, recv_sem):
        return pltpu.make_async_remote_copy(
            src_ref=ref.at[pl.ds(0, peers - 1)], dst_ref=ref.at[pl.ds(0, peers - 1)],
            send_sem=send_sem, recv_sem=recv_sem,
            device_id=peer_id(1), device_id_type=MESH,
        )

    def place(k):
        code = looked_up(table, ys * zs, k)
        dy = code // zs + low_y
        dz = lax.rem(code, zs) + low_z
        y = lax.rem(my_y + dy + ys, ys)
        z = lax.rem(my_z + dz + zs, zs)
        return dy, dz, y * zs + z

    def relay(k):
        dy, dz, block = place(k)
        star_copy(block, 0).wait_recv()

        @pl.when((dz == 0) & (dy > 0) & (dy < high_y))
        def _():
            star_copy(block, 0).start()

        @pl.when((dz == 0) & (dy < 0) & (dy > low_y))
        def _():
            star_copy(block, 1).start()

        @pl.when((dz >= 0) & (dz < high_z))
        def _():
            star_copy(block, 2).start()

        @pl.when((dz <= 0) & (dz > low_z))
        def _():
            star_copy(block, 3).start()

    for k in range(1, peers):
        sink_copy(k).start()
    for side in range(4):
        star_copy(home, side).start()
    early = 5

    def relay_early(k, _):
        relay(k)
        return 0

    lax.fori_loop(1, early, relay_early, 0)
    all_but_me(sink_ref, sink_send, sink_recv).wait_recv()

    def core_state(core):
        state = sink_ref[core * xs]
        for x in range(1, xs):
            state = state + sink_ref[core * xs + x]
        return state

    for core in range(cores):
        columns = jnp.transpose(core_state(core))
        for c in range(6):
            wide_ref[c, core * group : (core + 1) * group, :] = jnp.broadcast_to(
                columns[:, c : c + 1], (group, 128)
            )

    def compute(*accumulators):
        plain_acc = accumulators[:tiles]
        cross_acc = accumulators[tiles:]

        def one_block(k, _):
            buffer = lax.rem(k, 2)
            pltpu.matmul_push_rhs(
                plain_ref[buffer], staging_register=0, mxu_index=0, transpose=True
            )
            pltpu.matmul_push_rhs(
                cross_ref[buffer], staging_register=0, mxu_index=1, transpose=True
            )

            @pl.when((k + 2 >= early) & (k + 2 < blocks))
            def _():
                relay(k + 2)

            _, _, block = place(k)
            state = star_ref[block]
            _, _, following = place(jnp.minimum(k + 1, blocks - 1))
            star_weights(following, 1 - buffer)
            for step in range(tiles):
                rows = slice(step * tile, (step + 1) * tile)
                sinks = [wide_ref[c, rows, :] for c in range(6)]
                sinks = [jnp.concatenate([value] * (stars // 128), axis=1) for value in sinks]
                sep = [state[c : c + 1] - sinks[c] for c in range(3)]
                rel = [state[3 + c : 4 + c] - sinks[3 + c] for c in range(3)]
                radius_sq = sep[0] * sep[0] + (sep[1] * sep[1] + (sep[2] * sep[2] + SOFTENING))
                radial = sep[0] * rel[0] + sep[1] * rel[1] + sep[2] * rel[2]
                inverse = lax.rsqrt(radius_sq)
                inverse_sq = inverse * inverse
                cube = inverse_sq * inverse
                fifth = (cube * inverse_sq) * radial
                load = 0 if step == 0 else None
                high, low = split2(cube)
                pltpu.matmul_acc_lhs(plain_acc[step], high, load_staged_rhs=load)
                pltpu.matmul_acc_lhs(plain_acc[step], low)
                high, low = split2(fifth)
                pltpu.matmul_acc_lhs(cross_acc[step], high, load_staged_rhs=load)
                pltpu.matmul_acc_lhs(cross_acc[step], low)
            return 0

        lax.fori_loop(0, blocks, one_block, 0)
        for core in range(cores):
            sums = [
                (pltpu.matmul_pop(plain_acc[t]) + pltpu.matmul_pop(cross_acc[t]))[:, :128]
                for t in range(core * half_tiles, (core + 1) * half_tiles)
            ]
            rows = jnp.transpose(jnp.concatenate(sums, axis=0))
            state = core_state(core)
            pos = state[0:3]
            vel = state[3:6]
            whole = rows[18:19] + rows[19:20] + rows[20:21]
            cross = rows[21:22] + rows[22:23] + rows[23:24]
            new_acc = (rows[0:3] + rows[3:6] + rows[6:9]) - pos * whole
            new_jerk = (rows[9:12] + rows[12:15] + rows[15:18]) - vel * whole + pos * cross
            part_ref[core] = jnp.concatenate(
                [new_acc, new_jerk, jnp.zeros((2, group), F32)], axis=0
            )

    pl.run_scoped(
        compute,
        *[pltpu.ACC(0)((tile, 256), F32) for _ in range(tiles)],
        *[pltpu.ACC(1)((tile, 256), F32) for _ in range(tiles)],
    )
    for k in range(1, peers):
        part_copy(k).start()
    sum_ref[me] = part_ref[my_core]
    all_but_me(sink_ref, sink_send, sink_recv).wait_send()
    counts = (high_y, -low_y, ys * high_z, -ys * low_z)
    for side in range(4):
        pltpu.make_async_remote_copy(
            src_ref=star_ref.at[pl.ds(0, counts[side])], dst_ref=star_ref.at[pl.ds(0, counts[side])],
            send_sem=star_send.at[side], recv_sem=star_recv.at[0],
            device_id=side_id(*sides[side]), device_id_type=MESH,
        ).wait_send()
    all_but_me(sum_ref, part_send, part_recv).wait_recv()

    total = sum_ref[0]
    for k in range(1, peers):
        total = total + sum_ref[k]
    total = jnp.where(lane_x == my_x, total, 0.0)
    rows = total[:, :slots]
    for x in range(1, xs):
        rows = rows + total[:, x * slots : (x + 1) * slots]
    own_rows = own_ref[...]
    is_live = lax.broadcasted_iota(jnp.int32, (1, slots), 1) < count_ref[...]
    out_ref[...] = correct(own_rows[0:6], own_rows[6:9], own_rows[9:12], rows, is_live)
    all_but_me(sum_ref, part_send, part_recv).wait_send()


def solution(mesh):
    teams = mesh.shape["team"]
    cuts = mesh.shape["cuts"]
    xs = 4
    cores = 2
    blocks = teams * cuts // (xs * cores)

    def local(position, velocity, accel_old, jerk_old, star_mass, active_index, active_count):
        stars = position.shape[1]
        slots = active_index.shape[0]
        group = xs * slots
        vmem = pl.BlockSpec(memory_space=pltpu.VMEM)
        dma = pltpu.SemaphoreType.DMA
        return pl.pallas_call(
            functools.partial(step_kernel, teams, cuts, xs, slots, stars, cores),
            out_shape=jax.ShapeDtypeStruct((12, slots), F32),
            in_specs=[vmem] * 7,
            out_specs=vmem,
            scratch_shapes=[
                pltpu.VMEM((16, slots), F32),
                pltpu.VMEM((blocks, 8, stars), F32),
                pltpu.VMEM((xs * cores, 8, group), F32),
                pltpu.VMEM((cores, 8, group), F32),
                pltpu.VMEM((xs * cores, 8, group), F32),
                pltpu.VMEM((2, 256, stars), BF16),
                pltpu.VMEM((2, 256, stars), BF16),
                pltpu.VMEM((6, cores * group, 128), F32),
                dma((4,)), dma((blocks,)), dma, dma, dma, dma,
            ],
            compiler_params=pltpu.CompilerParams(collective_id=0, has_side_effects=True),
            name="hermite_step",
        )(
            position, velocity, accel_old, jerk_old,
            star_mass.reshape(1, stars), active_index.reshape(1, slots), active_count.reshape(1, 1),
        )

    column = P(None, ("team", "cuts"))
    line = P(("team", "cuts"))
    return jax.shard_map(
        local, mesh=mesh, in_specs=(column, column, column, column, line, line, line),
        out_specs=column, check_vma=False,
    )
```

```python
import functools

import jax
import jax.numpy as jnp
from jax import lax
from jax.experimental import pallas as pl
from jax.experimental.pallas import tpu as pltpu
from jax.sharding import PartitionSpec as P

STEP_DT = 0.5
SOFTENING = 0.0004
MESH = pl.DeviceIdType.MESH
F32 = jnp.float32
BF16 = jnp.bfloat16


def split2(value):
    high = value.astype(BF16)
    return high, (value - high.astype(F32)).astype(BF16)


def split3(value):
    high = value.astype(BF16)
    rest = value - high.astype(F32)
    middle = rest.astype(BF16)
    return high, middle, (rest - middle.astype(F32)).astype(BF16)


def stack_pieces(rows, height):
    filled = sum(row.shape[0] for row in rows)
    rows = [row.astype(F32) for row in rows]
    rows = rows + [jnp.zeros((height - filled, rows[0].shape[1]), F32)]
    return jnp.concatenate(rows, axis=0).astype(BF16)


def predict(position, velocity, accel_old, jerk_old):
    pred_pos = position + STEP_DT * (
        velocity + STEP_DT * (accel_old * 0.5 + STEP_DT * (jerk_old * (1.0 / 6.0)))
    )
    pred_vel = velocity + STEP_DT * (accel_old + STEP_DT * (jerk_old * 0.5))
    return (pred_pos, pred_vel)


def correct(sink_state, old_acc, old_jerk, new_rows, is_live):
    pred_pos = sink_state[:3]
    pred_vel = sink_state[3:6]
    new_acc = new_rows[:3]
    new_jerk = new_rows[3:6]
    change = old_acc - new_acc
    second = -6.0 * change - STEP_DT * (4.0 * old_jerk + 2.0 * new_jerk)
    third = 12.0 * change + 6.0 * STEP_DT * (old_jerk + new_jerk)
    new_pos = pred_pos + STEP_DT * STEP_DT * (second * (1.0 / 24.0) + third * (1.0 / 120.0))
    new_vel = pred_vel + STEP_DT * (second * (1.0 / 6.0) + third * (1.0 / 24.0))
    stacked = jnp.concatenate([new_pos, new_vel, new_acc, new_jerk], axis=0)
    return jnp.where(is_live, stacked, 0.0)


def step_kernel(
    teams, cuts, xs, slots, stars, cores,
    pos_ref, vel_ref, acc_ref, jerk_ref, mass_ref, index_ref, count_ref, out_ref,
    own_ref, star_ref, sink_ref, part_ref, sum_ref, plain_ref, cross_ref, wide_ref,
    row_recv, half_recv, side_send, sink_send, sink_recv, part_send, part_recv,
):
    team = lax.axis_index("team")
    cut = lax.axis_index("cuts")
    zs = cuts // xs
    ys = teams // cores
    my_y = team >> 1
    my_core = team & 1
    my_z = cut >> 2
    my_x = cut & 3
    group = xs * slots
    peers = cores * xs
    tile = 16
    half_tiles = group // tile
    tiles = cores * half_tiles
    me = my_core * xs + my_x
    half = ys // 2
    units = 2 * (zs - 1)
    paired = units - 2

    peer_steps = [(dc, dx) for dc in range(cores) for dx in range(xs)][1:]

    def peer_id(step):
        dc, dx = step
        return (my_y * cores + ((my_core + dc) & 1), my_z * xs + ((my_x + dx) & 3))

    def side_id(dy, dz):
        y = (my_y + dy) & (ys - 1)
        z = (my_z + dz) & (zs - 1)
        return (y * cores + my_core, z * xs + my_x)

    sides = ((-1, 0), (1, 0), (0, -1), (0, 1))
    barrier = pltpu.get_barrier_semaphore()
    for dy, dz in sides:
        pl.semaphore_signal(barrier, inc=1, device_id=side_id(dy, dz), device_id_type=MESH)
    for step in peer_steps:
        pl.semaphore_signal(barrier, inc=1, device_id=peer_id(step), device_id_type=MESH)

    acc_old = acc_ref[...]
    jerk_old = jerk_ref[...]
    pred_pos, pred_vel = predict(pos_ref[...], vel_ref[...], acc_old, jerk_old)
    weight = mass_ref[...] * (1.0 / (stars * teams * cuts))
    home = my_z * ys + my_y
    star_ref[home] = jnp.concatenate(
        [pred_pos, pred_vel, weight, jnp.zeros((1, stars), F32)], axis=0
    )
    index = jnp.concatenate(
        [index_ref[...], jnp.full((1, 256 - slots), -1, jnp.int32)], axis=1
    )
    picked = (
        lax.broadcasted_iota(jnp.int32, (stars, 256), 0) == index
    ).astype(F32).astype(BF16)
    source = jnp.concatenate([pred_pos, pred_vel, acc_old, jerk_old, jnp.zeros((4, stars), F32)], 0)

    def pick(pick_acc):
        pltpu.matmul_push_rhs(picked, staging_register=0, mxu_index=0)
        for n, piece in enumerate(split3(source)):
            pltpu.matmul_acc_lhs(pick_acc, piece, load_staged_rhs=0 if n == 0 else None)
        own_ref[...] = pltpu.matmul_pop(pick_acc)[:, :slots]

    pl.run_scoped(pick, pltpu.ACC(0)((16, 256), F32))
    own = own_ref[...]
    lane_x = lax.broadcasted_iota(jnp.int32, (8, group), 1) // slots
    state = jnp.concatenate([own[0:6], jnp.zeros((2, slots), F32)], axis=0)
    sink_ref[me] = jnp.where(lane_x == my_x, jnp.concatenate([state] * xs, axis=1), 0.0)

    def star_weights(block, buffer):
        state = star_ref[block]
        mass = state[6:7]
        mass_pos = mass * state[0:3]
        mass_vel = mass * state[3:6]
        empty3 = jnp.zeros((3, stars), F32)
        empty9 = jnp.zeros((9, stars), F32)
        plain_ref[buffer, :32, :] = stack_pieces(
            [*split3(mass_pos), *split3(mass_vel), *split3(mass), empty3], 32
        )
        cross_ref[buffer, :32, :] = stack_pieces(
            [empty9, *split3(-3.0 * mass_pos), empty3, *split3(3.0 * mass)], 32
        )

    plain_ref[...] = jnp.zeros_like(plain_ref)
    cross_ref[...] = jnp.zeros_like(cross_ref)
    star_weights(home, 0)

    pl.semaphore_wait(barrier, len(sides) + len(peer_steps))

    def sink_copy(step):
        return pltpu.make_async_remote_copy(
            src_ref=sink_ref.at[me], dst_ref=sink_ref.at[me],
            send_sem=sink_send, recv_sem=sink_recv,
            device_id=peer_id(step), device_id_type=MESH,
        )

    def part_copy(step):
        return pltpu.make_async_remote_copy(
            src_ref=part_ref.at[(my_core + step[0]) & 1], dst_ref=sum_ref.at[me],
            send_sem=part_send, recv_sem=part_recv,
            device_id=peer_id(step), device_id_type=MESH,
        )

    def row_copy(block, side, number):
        return pltpu.make_async_remote_copy(
            src_ref=star_ref.at[block], dst_ref=star_ref.at[block],
            send_sem=side_send.at[side], recv_sem=row_recv.at[number],
            device_id=side_id(*sides[side]), device_id_type=MESH,
        )

    def half_copy(block, side, unit, device):
        return pltpu.make_async_remote_copy(
            src_ref=star_ref.at[block], dst_ref=star_ref.at[block],
            send_sem=side_send.at[side], recv_sem=half_recv.at[unit],
            device_id=device, device_id_type=MESH,
        )

    def many(ref, count, send_sem, recv_sem):
        return pltpu.make_async_remote_copy(
            src_ref=ref.at[pl.ds(0, count)], dst_ref=ref.at[pl.ds(0, count)],
            send_sem=send_sem, recv_sem=recv_sem,
            device_id=side_id(0, 1), device_id_type=MESH,
        )

    row = [(n + 1) // 2 * (1 if n & 1 else -1) for n in range(ys)]
    high_y, low_y = max(row), min(row)
    high_z, low_z = zs // 2, -((zs - 1) // 2)

    def row_block(n):
        return my_z * ys + ((my_y + row[n]) & (ys - 1))

    def pass_on(n):
        block = row_block(n)
        dy = row[n]
        if 0 <= dy < high_y:
            row_copy(block, 0, row.index(dy + 1)).start()
        if low_y < dy <= 0:
            row_copy(block, 1, row.index(dy - 1)).start()
        part = n // half
        half_copy(block, 2, 2 * part, side_id(*sides[2])).start()
        half_copy(block, 3, 2 * part + 1, side_id(*sides[3])).start()

    def take_row(n):
        row_copy(row_block(n), 0, n).wait_recv()
        pass_on(n)

    def unit_place(unit):
        last = unit >= paired
        distance = (unit >> 2) + 1
        back = jnp.where(last, 0, unit & 1)
        part = jnp.where(last, unit & 1, (unit >> 1) & 1)
        dz = jnp.where(back == 1, -distance, distance)
        return distance, back, part, (my_z + dz) & (zs - 1)

    def unit_block(part, z, n):
        number = part * half + n
        dy = ((number + 1) >> 1) * (2 * (number & 1) - 1)
        return z * ys + ((my_y + dy) & (ys - 1))

    def take_unit(unit):
        many(star_ref, half, side_send.at[0], half_recv.at[unit]).wait_recv()
        distance, back, part, z = unit_place(unit)
        following = jnp.where(unit < paired - 4, unit + 4, paired + part)
        for side in (2, 3):
            reach = high_z if side == 2 else -low_z

            @pl.when((back == side - 2) & (distance < reach))
            def _():
                for n in range(half):
                    half_copy(
                        unit_block(part, z, n), side, following, side_id(*sides[side])
                    ).start()

    for step in peer_steps:
        sink_copy(step).start()
    pass_on(0)
    take_row(1)
    take_row(2)
    many(sink_ref, peers - 1, sink_send, sink_recv).wait_recv()

    def core_state(core):
        state = sink_ref[core * xs]
        for x in range(1, xs):
            state = state + sink_ref[core * xs + x]
        return state

    for core in range(cores):
        columns = jnp.transpose(core_state(core))
        for c in range(6):
            wide_ref[c, core * group : (core + 1) * group, :] = jnp.broadcast_to(
                columns[:, c : c + 1], (group, 128)
            )

    def compute(*accumulators):
        plain_acc = accumulators[:tiles]
        cross_acc = accumulators[tiles:]

        def pairs(block, buffer, following):
            pltpu.matmul_push_rhs(
                plain_ref[buffer], staging_register=0, mxu_index=0, transpose=True
            )
            pltpu.matmul_push_rhs(
                cross_ref[buffer], staging_register=0, mxu_index=1, transpose=True
            )
            state = star_ref[block]
            star_weights(following, 1 - buffer)
            for step in range(tiles):
                rows = slice(step * tile, (step + 1) * tile)
                sinks = [wide_ref[c, rows, :] for c in range(6)]
                sinks = [jnp.concatenate([value] * (stars // 128), axis=1) for value in sinks]
                sep = [state[c : c + 1] - sinks[c] for c in range(3)]
                rel = [state[3 + c : 4 + c] - sinks[3 + c] for c in range(3)]
                radius_sq = sep[0] * sep[0] + (sep[1] * sep[1] + (sep[2] * sep[2] + SOFTENING))
                radial = sep[0] * rel[0] + sep[1] * rel[1] + sep[2] * rel[2]
                inverse = lax.rsqrt(radius_sq)
                inverse_sq = inverse * inverse
                cube = inverse_sq * inverse
                fifth = (cube * inverse_sq) * radial
                load = 0 if step == 0 else None
                high, low = split2(cube)
                pltpu.matmul_acc_lhs(plain_acc[step], high, load_staged_rhs=load)
                pltpu.matmul_acc_lhs(plain_acc[step], low)
                high, low = split2(fifth)
                pltpu.matmul_acc_lhs(cross_acc[step], high, load_staged_rhs=load)
                pltpu.matmul_acc_lhs(cross_acc[step], low)

        for n in range(ys):
            if n & 1 and n + 2 < ys:
                take_row(n + 2)
                if n + 3 < ys:
                    take_row(n + 3)
            if n + 1 == ys:
                take_unit(0)
                _, _, part, z = unit_place(0)
                following = unit_block(part, z, 0)
            else:
                following = row_block(n + 1)
            pairs(row_block(n), n & 1, following)

        def one_unit(unit, _):
            @pl.when(unit + 1 < units)
            def _():
                take_unit(unit + 1)

            _, _, part, z = unit_place(unit)
            _, _, next_part, next_z = unit_place(jnp.minimum(unit + 1, units - 1))
            for n in range(half):
                block = unit_block(part, z, n)
                if n + 1 < half:
                    following = unit_block(part, z, n + 1)
                else:
                    following = unit_block(next_part, next_z, 0)
                pairs(block, n & 1, following)
            return 0

        lax.fori_loop(0, units, one_unit, 0)
        for core in range(cores):
            sums = [
                (pltpu.matmul_pop(plain_acc[t]) + pltpu.matmul_pop(cross_acc[t]))[:, :128]
                for t in range(core * half_tiles, (core + 1) * half_tiles)
            ]
            rows = jnp.transpose(jnp.concatenate(sums, axis=0))
            state = core_state(core)
            pos = state[0:3]
            vel = state[3:6]
            whole = rows[18:19] + rows[19:20] + rows[20:21]
            cross = rows[21:22] + rows[22:23] + rows[23:24]
            new_acc = (rows[0:3] + rows[3:6] + rows[6:9]) - pos * whole
            new_jerk = (rows[9:12] + rows[12:15] + rows[15:18]) - vel * whole + pos * cross
            part_ref[core] = jnp.concatenate(
                [new_acc, new_jerk, jnp.zeros((2, group), F32)], axis=0
            )

    pl.run_scoped(
        compute,
        *[pltpu.ACC(0)((tile, 256), F32) for _ in range(tiles)],
        *[pltpu.ACC(1)((tile, 256), F32) for _ in range(tiles)],
    )
    for step in peer_steps:
        part_copy(step).start()
    sum_ref[me] = part_ref[my_core]
    many(sink_ref, peers - 1, sink_send, sink_recv).wait_send()
    for side, count in enumerate((high_y, -low_y, ys * high_z, -ys * low_z)):
        many(star_ref, count, side_send.at[side], row_recv.at[0]).wait_send()
    many(sum_ref, peers - 1, part_send, part_recv).wait_recv()

    total = sum_ref[0]
    for k in range(1, peers):
        total = total + sum_ref[k]
    total = jnp.where(lane_x == my_x, total, 0.0)
    rows = total[:, :slots]
    for x in range(1, xs):
        rows = rows + total[:, x * slots : (x + 1) * slots]
    own_rows = own_ref[...]
    is_live = lax.broadcasted_iota(jnp.int32, (1, slots), 1) < count_ref[...]
    out_ref[...] = correct(own_rows[0:6], own_rows[6:9], own_rows[9:12], rows, is_live)
    many(sum_ref, peers - 1, part_send, part_recv).wait_send()


def solution(mesh):
    teams = mesh.shape["team"]
    cuts = mesh.shape["cuts"]
    xs = 4
    cores = 2
    blocks = teams * cuts // (xs * cores)

    def local(position, velocity, accel_old, jerk_old, star_mass, active_index, active_count):
        stars = position.shape[1]
        slots = active_index.shape[0]
        group = xs * slots
        vmem = pl.BlockSpec(memory_space=pltpu.VMEM)
        dma = pltpu.SemaphoreType.DMA
        return pl.pallas_call(
            functools.partial(step_kernel, teams, cuts, xs, slots, stars, cores),
            out_shape=jax.ShapeDtypeStruct((12, slots), F32),
            in_specs=[vmem] * 7,
            out_specs=vmem,
            scratch_shapes=[
                pltpu.VMEM((16, slots), F32),
                pltpu.VMEM((blocks, 8, stars), F32),
                pltpu.VMEM((xs * cores, 8, group), F32),
                pltpu.VMEM((cores, 8, group), F32),
                pltpu.VMEM((xs * cores, 8, group), F32),
                pltpu.VMEM((2, 256, stars), BF16),
                pltpu.VMEM((2, 256, stars), BF16),
                pltpu.VMEM((6, cores * group, 128), F32),
                dma((teams // cores,)), dma((2 * (cuts // xs - 1),)), dma((4,)), dma, dma, dma, dma,
            ],
            compiler_params=pltpu.CompilerParams(collective_id=0, has_side_effects=True),
            name="hermite_step",
        )(
            position, velocity, accel_old, jerk_old,
            star_mass.reshape(1, stars), active_index.reshape(1, slots), active_count.reshape(1, 1),
        )

    column = P(None, ("team", "cuts"))
    line = P(("team", "cuts"))
    return jax.shard_map(
        local, mesh=mesh, in_specs=(column, column, column, column, line, line, line),
        out_specs=column, check_vma=False,
    )
```

```python
import functools

import jax
import jax.numpy as jnp
from jax import lax
from jax.experimental import pallas as pl
from jax.experimental.pallas import tpu as pltpu
from jax.sharding import PartitionSpec as P

STEP_DT = 0.5
SOFTENING = 0.0004
MESH = pl.DeviceIdType.MESH
F32 = jnp.float32
BF16 = jnp.bfloat16


def split2(value):
    high = value.astype(BF16)
    return high, (value - high.astype(F32)).astype(BF16)


def split3(value):
    high = value.astype(BF16)
    rest = value - high.astype(F32)
    middle = rest.astype(BF16)
    return high, middle, (rest - middle.astype(F32)).astype(BF16)


def stack_pieces(rows, height):
    filled = sum(row.shape[0] for row in rows)
    rows = [row.astype(F32) for row in rows]
    rows = rows + [jnp.zeros((height - filled, rows[0].shape[1]), F32)]
    return jnp.concatenate(rows, axis=0).astype(BF16)


def predict(position, velocity, accel_old, jerk_old):
    pred_pos = position + STEP_DT * (
        velocity + STEP_DT * (accel_old * 0.5 + STEP_DT * (jerk_old * (1.0 / 6.0)))
    )
    pred_vel = velocity + STEP_DT * (accel_old + STEP_DT * (jerk_old * 0.5))
    return (pred_pos, pred_vel)


def correct(sink_state, old_acc, old_jerk, new_rows, is_live):
    pred_pos = sink_state[:3]
    pred_vel = sink_state[3:6]
    new_acc = new_rows[:3]
    new_jerk = new_rows[3:6]
    change = old_acc - new_acc
    second = -6.0 * change - STEP_DT * (4.0 * old_jerk + 2.0 * new_jerk)
    third = 12.0 * change + 6.0 * STEP_DT * (old_jerk + new_jerk)
    new_pos = pred_pos + STEP_DT * STEP_DT * (second * (1.0 / 24.0) + third * (1.0 / 120.0))
    new_vel = pred_vel + STEP_DT * (second * (1.0 / 6.0) + third * (1.0 / 24.0))
    stacked = jnp.concatenate([new_pos, new_vel, new_acc, new_jerk], axis=0)
    return jnp.where(is_live, stacked, 0.0)


def step_kernel(
    teams, cuts, xs, slots, stars, cores,
    pos_ref, vel_ref, acc_ref, jerk_ref, mass_ref, index_ref, count_ref, out_ref,
    own_ref, star_ref, sink_ref, part_ref, sum_ref, plain_ref, cross_ref, wide_ref,
    row_recv, half_recv, row_send, half_send, sink_send, sink_recv, part_send, part_recv,
):
    team = lax.axis_index("team")
    cut = lax.axis_index("cuts")
    side = teams // cores
    my_y = team >> 1
    my_core = team & 1
    my_z = cut >> 2
    my_x = cut & 3
    first = jnp.where(my_core == 0, my_y, my_z)
    second = jnp.where(my_core == 0, my_z, my_y)
    group = xs * slots
    peers = cores * xs
    tile = 16
    half_tiles = group // tile
    tiles = cores * half_tiles
    me = my_core * xs + my_x
    half = side // 2
    units = 2 * (side - 1)
    paired = units - 2

    peer_steps = [(dc, dx) for dc in range(cores) for dx in range(xs)][1:]

    def peer_id(step):
        dc, dx = step
        return (my_y * cores + ((my_core + dc) & 1), my_z * xs + ((my_x + dx) & 3))

    def ring_id(d_first, d_second):
        u = (first + d_first) & (side - 1)
        w = (second + d_second) & (side - 1)
        y = jnp.where(my_core == 0, u, w)
        z = jnp.where(my_core == 0, w, u)
        return (y * cores + my_core, z * xs + my_x)

    row = [(n + 1) // 2 * (1 if n & 1 else -1) for n in range(side)]
    barrier = pltpu.get_barrier_semaphore()
    for offset in row[1:]:
        pl.semaphore_signal(barrier, inc=1, device_id=ring_id(offset, 0), device_id_type=MESH)
        pl.semaphore_signal(barrier, inc=1, device_id=ring_id(0, offset), device_id_type=MESH)
    for step in peer_steps:
        pl.semaphore_signal(barrier, inc=1, device_id=peer_id(step), device_id_type=MESH)

    acc_old = acc_ref[...]
    jerk_old = jerk_ref[...]
    pred_pos, pred_vel = predict(pos_ref[...], vel_ref[...], acc_old, jerk_old)
    weight = mass_ref[...] * (1.0 / (stars * teams * cuts))
    home = second * side + first
    star_ref[home] = jnp.concatenate(
        [pred_pos, pred_vel, weight, jnp.zeros((1, stars), F32)], axis=0
    )
    index = jnp.concatenate(
        [index_ref[...], jnp.full((1, 256 - slots), -1, jnp.int32)], axis=1
    )
    picked = (
        lax.broadcasted_iota(jnp.int32, (stars, 256), 0) == index
    ).astype(F32).astype(BF16)
    source = jnp.concatenate([pred_pos, pred_vel, acc_old, jerk_old, jnp.zeros((4, stars), F32)], 0)

    def pick(pick_acc):
        pltpu.matmul_push_rhs(picked, staging_register=0, mxu_index=0)
        for n, piece in enumerate(split3(source)):
            pltpu.matmul_acc_lhs(pick_acc, piece, load_staged_rhs=0 if n == 0 else None)
        own_ref[...] = pltpu.matmul_pop(pick_acc)[:, :slots]

    pl.run_scoped(pick, pltpu.ACC(0)((16, 256), F32))
    own = own_ref[...]
    lane_x = lax.broadcasted_iota(jnp.int32, (8, group), 1) // slots
    state = jnp.concatenate([own[0:6], jnp.zeros((2, slots), F32)], axis=0)
    sink_ref[me] = jnp.where(lane_x == my_x, jnp.concatenate([state] * xs, axis=1), 0.0)

    def star_weights(block, buffer):
        state = star_ref[block]
        mass = state[6:7]
        mass_pos = mass * state[0:3]
        mass_vel = mass * state[3:6]
        empty3 = jnp.zeros((3, stars), F32)
        empty9 = jnp.zeros((9, stars), F32)
        plain_ref[buffer, :32, :] = stack_pieces(
            [*split3(mass_pos), *split3(mass_vel), *split3(mass), empty3], 32
        )
        cross_ref[buffer, :32, :] = stack_pieces(
            [empty9, *split3(-3.0 * mass_pos), empty3, *split3(3.0 * mass)], 32
        )

    plain_ref[...] = jnp.zeros_like(plain_ref)
    cross_ref[...] = jnp.zeros_like(cross_ref)
    star_weights(home, 0)

    pl.semaphore_wait(barrier, 2 * (side - 1) + len(peer_steps))

    def sink_copy(step):
        return pltpu.make_async_remote_copy(
            src_ref=sink_ref.at[me], dst_ref=sink_ref.at[me],
            send_sem=sink_send, recv_sem=sink_recv,
            device_id=peer_id(step), device_id_type=MESH,
        )

    def part_copy(step):
        return pltpu.make_async_remote_copy(
            src_ref=part_ref.at[(my_core + step[0]) & 1], dst_ref=sum_ref.at[me],
            send_sem=part_send, recv_sem=part_recv,
            device_id=peer_id(step), device_id_type=MESH,
        )

    def row_copy(block, number, offset):
        return pltpu.make_async_remote_copy(
            src_ref=star_ref.at[block], dst_ref=star_ref.at[block],
            send_sem=row_send, recv_sem=row_recv.at[number],
            device_id=ring_id(offset, 0), device_id_type=MESH,
        )

    def half_copy(block, unit, offset):
        return pltpu.make_async_remote_copy(
            src_ref=star_ref.at[block], dst_ref=star_ref.at[block],
            send_sem=half_send, recv_sem=half_recv.at[unit],
            device_id=ring_id(0, offset), device_id_type=MESH,
        )

    def many(ref, count, send_sem, recv_sem):
        return pltpu.make_async_remote_copy(
            src_ref=ref.at[pl.ds(0, count)], dst_ref=ref.at[pl.ds(0, count)],
            send_sem=send_sem, recv_sem=recv_sem,
            device_id=peer_id((0, 1)), device_id_type=MESH,
        )

    def row_block(n):
        return second * side + ((first + row[n]) & (side - 1))

    def unit_of(offset, part):
        if offset == side // 2:
            return paired + part
        return 4 * (abs(offset) - 1) + 2 * part + (1 if offset < 0 else 0)

    def pass_on(n):
        block = row_block(n)
        for offset in row[1:]:
            seen = -offset if offset != side // 2 else offset
            half_copy(block, unit_of(seen, n // half), offset).start()

    def take_row(n):
        row_copy(row_block(n), n, row[1]).wait_recv()
        pass_on(n)

    def unit_place(unit):
        last = unit >= paired
        distance = (unit >> 2) + 1
        back = jnp.where(last, 0, unit & 1)
        part = jnp.where(last, unit & 1, (unit >> 1) & 1)
        offset = jnp.where(back == 1, -distance, distance)
        return part, (second + offset) & (side - 1)

    def unit_block(part, w, n):
        number = part * half + n
        offset = ((number + 1) >> 1) * (2 * (number & 1) - 1)
        return w * side + ((first + offset) & (side - 1))

    def take_unit(unit):
        many(star_ref, half, half_send, half_recv.at[unit]).wait_recv()

    for step in peer_steps:
        sink_copy(step).start()
    for n in range(1, side):
        seen = -row[n] if row[n] != side // 2 else row[n]
        row_copy(home, row.index(seen), row[n]).start()
    pass_on(0)
    for n in range(1, 5):
        take_row(n)
    many(sink_ref, peers - 1, sink_send, sink_recv).wait_recv()

    def core_state(core):
        state = sink_ref[core * xs]
        for x in range(1, xs):
            state = state + sink_ref[core * xs + x]
        return state

    for core in range(cores):
        columns = jnp.transpose(core_state(core))
        for c in range(6):
            wide_ref[c, core * group : (core + 1) * group, :] = jnp.broadcast_to(
                columns[:, c : c + 1], (group, 128)
            )

    def compute(*accumulators):
        plain_acc = accumulators[:tiles]
        cross_acc = accumulators[tiles:]

        def pairs(block, buffer, following):
            pltpu.matmul_push_rhs(
                plain_ref[buffer], staging_register=0, mxu_index=0, transpose=True
            )
            pltpu.matmul_push_rhs(
                cross_ref[buffer], staging_register=0, mxu_index=1, transpose=True
            )
            state = star_ref[block]
            star_weights(following, 1 - buffer)
            for step in range(tiles):
                rows = slice(step * tile, (step + 1) * tile)
                sinks = [wide_ref[c, rows, :] for c in range(6)]
                sinks = [jnp.concatenate([value] * (stars // 128), axis=1) for value in sinks]
                sep = [state[c : c + 1] - sinks[c] for c in range(3)]
                rel = [state[3 + c : 4 + c] - sinks[3 + c] for c in range(3)]
                radius_sq = sep[0] * sep[0] + (sep[1] * sep[1] + (sep[2] * sep[2] + SOFTENING))
                radial = sep[0] * rel[0] + sep[1] * rel[1] + sep[2] * rel[2]
                inverse = lax.rsqrt(radius_sq)
                inverse_sq = inverse * inverse
                cube = inverse_sq * inverse
                fifth = (cube * inverse_sq) * radial
                load = 0 if step == 0 else None
                high, low = split2(cube)
                pltpu.matmul_acc_lhs(plain_acc[step], high, load_staged_rhs=load)
                pltpu.matmul_acc_lhs(plain_acc[step], low)
                high, low = split2(fifth)
                pltpu.matmul_acc_lhs(cross_acc[step], high, load_staged_rhs=load)
                pltpu.matmul_acc_lhs(cross_acc[step], low)

        for n in range(side):
            if n == 1:
                take_row(5)
                take_row(6)
            if n == 3:
                take_row(7)
            if n + 1 == side:
                take_unit(0)
                part, w = unit_place(0)
                following = unit_block(part, w, 0)
            else:
                following = row_block(n + 1)
            pairs(row_block(n), n & 1, following)

        def one_unit(unit, _):
            @pl.when(unit + 1 < units)
            def _():
                take_unit(unit + 1)

            part, w = unit_place(unit)
            next_part, next_w = unit_place(jnp.minimum(unit + 1, units - 1))
            for n in range(half):
                block = unit_block(part, w, n)
                if n + 1 < half:
                    following = unit_block(part, w, n + 1)
                else:
                    following = unit_block(next_part, next_w, 0)
                pairs(block, n & 1, following)
            return 0

        lax.fori_loop(0, units, one_unit, 0)
        for core in range(cores):
            sums = [
                (pltpu.matmul_pop(plain_acc[t]) + pltpu.matmul_pop(cross_acc[t]))[:, :128]
                for t in range(core * half_tiles, (core + 1) * half_tiles)
            ]
            rows = jnp.transpose(jnp.concatenate(sums, axis=0))
            state = core_state(core)
            pos = state[0:3]
            vel = state[3:6]
            whole = rows[18:19] + rows[19:20] + rows[20:21]
            cross = rows[21:22] + rows[22:23] + rows[23:24]
            new_acc = (rows[0:3] + rows[3:6] + rows[6:9]) - pos * whole
            new_jerk = (rows[9:12] + rows[12:15] + rows[15:18]) - vel * whole + pos * cross
            part_ref[core] = jnp.concatenate(
                [new_acc, new_jerk, jnp.zeros((2, group), F32)], axis=0
            )

    pl.run_scoped(
        compute,
        *[pltpu.ACC(0)((tile, 256), F32) for _ in range(tiles)],
        *[pltpu.ACC(1)((tile, 256), F32) for _ in range(tiles)],
    )
    for step in peer_steps:
        part_copy(step).start()
    sum_ref[me] = part_ref[my_core]
    many(sink_ref, peers - 1, sink_send, sink_recv).wait_send()
    many(star_ref, side - 1, row_send, row_recv.at[0]).wait_send()
    many(star_ref, side * (side - 1), half_send, half_recv.at[0]).wait_send()
    many(sum_ref, peers - 1, part_send, part_recv).wait_recv()

    total = sum_ref[0]
    for k in range(1, peers):
        total = total + sum_ref[k]
    total = jnp.where(lane_x == my_x, total, 0.0)
    rows = total[:, :slots]
    for x in range(1, xs):
        rows = rows + total[:, x * slots : (x + 1) * slots]
    own_rows = own_ref[...]
    is_live = lax.broadcasted_iota(jnp.int32, (1, slots), 1) < count_ref[...]
    out_ref[...] = correct(own_rows[0:6], own_rows[6:9], own_rows[9:12], rows, is_live)
    many(sum_ref, peers - 1, part_send, part_recv).wait_send()


def solution(mesh):
    teams = mesh.shape["team"]
    cuts = mesh.shape["cuts"]
    xs = 4
    cores = 2
    blocks = teams * cuts // (xs * cores)

    def local(position, velocity, accel_old, jerk_old, star_mass, active_index, active_count):
        stars = position.shape[1]
        slots = active_index.shape[0]
        group = xs * slots
        vmem = pl.BlockSpec(memory_space=pltpu.VMEM)
        dma = pltpu.SemaphoreType.DMA
        return pl.pallas_call(
            functools.partial(step_kernel, teams, cuts, xs, slots, stars, cores),
            out_shape=jax.ShapeDtypeStruct((12, slots), F32),
            in_specs=[vmem] * 7,
            out_specs=vmem,
            scratch_shapes=[
                pltpu.VMEM((16, slots), F32),
                pltpu.VMEM((blocks, 8, stars), F32),
                pltpu.VMEM((xs * cores, 8, group), F32),
                pltpu.VMEM((cores, 8, group), F32),
                pltpu.VMEM((xs * cores, 8, group), F32),
                pltpu.VMEM((2, 256, stars), BF16),
                pltpu.VMEM((2, 256, stars), BF16),
                pltpu.VMEM((6, cores * group, 128), F32),
                dma((teams // cores,)), dma((2 * (cuts // xs - 1),)), dma, dma, dma, dma, dma, dma,
            ],
            compiler_params=pltpu.CompilerParams(collective_id=0, has_side_effects=True),
            name="hermite_step",
        )(
            position, velocity, accel_old, jerk_old,
            star_mass.reshape(1, stars), active_index.reshape(1, slots), active_count.reshape(1, 1),
        )

    column = P(None, ("team", "cuts"))
    line = P(("team", "cuts"))
    return jax.shard_map(
        local, mesh=mesh, in_specs=(column, column, column, column, line, line, line),
        out_specs=column, check_vma=False,
    )
```

```python
import functools

import jax
import jax.numpy as jnp
from jax import lax
from jax.experimental import pallas as pl
from jax.experimental.pallas import tpu as pltpu
from jax.sharding import PartitionSpec as P

STEP_DT = 0.5
SOFTENING = 0.0004
MESH = pl.DeviceIdType.MESH
F32 = jnp.float32
BF16 = jnp.bfloat16


def split2(value):
    high = value.astype(BF16)
    return high, (value - high.astype(F32)).astype(BF16)


def split3(value):
    high = value.astype(BF16)
    rest = value - high.astype(F32)
    middle = rest.astype(BF16)
    return high, middle, (rest - middle.astype(F32)).astype(BF16)


def stack_pieces(rows, height):
    filled = sum(row.shape[0] for row in rows)
    rows = [row.astype(F32) for row in rows]
    rows = rows + [jnp.zeros((height - filled, rows[0].shape[1]), F32)]
    return jnp.concatenate(rows, axis=0).astype(BF16)


def predict(position, velocity, accel_old, jerk_old):
    pred_pos = position + STEP_DT * (
        velocity + STEP_DT * (accel_old * 0.5 + STEP_DT * (jerk_old * (1.0 / 6.0)))
    )
    pred_vel = velocity + STEP_DT * (accel_old + STEP_DT * (jerk_old * 0.5))
    return (pred_pos, pred_vel)


def correct(sink_state, old_acc, old_jerk, new_rows, is_live):
    pred_pos = sink_state[:3]
    pred_vel = sink_state[3:6]
    new_acc = new_rows[:3]
    new_jerk = new_rows[3:6]
    change = old_acc - new_acc
    second = -6.0 * change - STEP_DT * (4.0 * old_jerk + 2.0 * new_jerk)
    third = 12.0 * change + 6.0 * STEP_DT * (old_jerk + new_jerk)
    new_pos = pred_pos + STEP_DT * STEP_DT * (second * (1.0 / 24.0) + third * (1.0 / 120.0))
    new_vel = pred_vel + STEP_DT * (second * (1.0 / 6.0) + third * (1.0 / 24.0))
    stacked = jnp.concatenate([new_pos, new_vel, new_acc, new_jerk], axis=0)
    return jnp.where(is_live, stacked, 0.0)


def step_kernel(
    teams, cuts, xs, slots, stars, cores,
    pos_hbm, vel_hbm, acc_hbm, jerk_hbm, mass_hbm, index_hbm, count_hbm, out_ref,
    pos_ref, vel_ref, acc_ref, jerk_ref, mass_ref, index_ref, count_ref, load_sem,
    own_ref, star_ref, sink_ref, part_ref, sum_ref, plain_ref, cross_ref, wide_ref,
    row_recv, half_recv, row_send, half_send, sink_send, sink_recv, part_send, part_recv,
):
    team = lax.axis_index("team")
    cut = lax.axis_index("cuts")
    side = teams // cores
    my_y = team >> 1
    my_core = team & 1
    my_z = cut >> 2
    my_x = cut & 3
    first = jnp.where(my_core == 0, my_y, my_z)
    second = jnp.where(my_core == 0, my_z, my_y)
    group = xs * slots
    peers = cores * xs
    tile = 16
    half_tiles = group // tile
    tiles = cores * half_tiles
    me = my_core * xs + my_x
    half = side // 2
    units = 2 * (side - 1)
    paired = units - 2

    peer_steps = [(dc, dx) for dc in range(cores) for dx in range(xs)][1:]

    def peer_id(step):
        dc, dx = step
        return (my_y * cores + ((my_core + dc) & 1), my_z * xs + ((my_x + dx) & 3))

    def ring_id(d_first, d_second):
        u = (first + d_first) & (side - 1)
        w = (second + d_second) & (side - 1)
        y = jnp.where(my_core == 0, u, w)
        z = jnp.where(my_core == 0, w, u)
        return (y * cores + my_core, z * xs + my_x)

    row = [(n + 1) // 2 * (1 if n & 1 else -1) for n in range(side)]
    barrier = pltpu.get_barrier_semaphore()
    for offset in row[1:]:
        pl.semaphore_signal(barrier, inc=1, device_id=ring_id(offset, 0), device_id_type=MESH)
        pl.semaphore_signal(barrier, inc=1, device_id=ring_id(0, offset), device_id_type=MESH)
    for step in peer_steps:
        pl.semaphore_signal(barrier, inc=1, device_id=peer_id(step), device_id_type=MESH)

    loads = [
        pltpu.make_async_copy(source, target, load_sem.at[n])
        for n, (source, target) in enumerate((
            (pos_hbm, pos_ref), (vel_hbm, vel_ref), (acc_hbm, acc_ref), (jerk_hbm, jerk_ref),
            (mass_hbm, mass_ref), (index_hbm, index_ref), (count_hbm, count_ref),
        ))
    ]
    for load in loads:
        load.start()
    plain_ref[...] = jnp.zeros_like(plain_ref)
    cross_ref[...] = jnp.zeros_like(cross_ref)
    for load in loads:
        load.wait()

    acc_old = acc_ref[...]
    jerk_old = jerk_ref[...]
    pred_pos, pred_vel = predict(pos_ref[...], vel_ref[...], acc_old, jerk_old)
    weight = mass_ref[...] * (1.0 / (stars * teams * cuts))
    home = second * side + first
    star_ref[home] = jnp.concatenate(
        [pred_pos, pred_vel, weight, jnp.zeros((1, stars), F32)], axis=0
    )
    index = jnp.concatenate(
        [index_ref[...], jnp.full((1, 256 - slots), -1, jnp.int32)], axis=1
    )
    picked = (
        lax.broadcasted_iota(jnp.int32, (stars, 256), 0) == index
    ).astype(F32).astype(BF16)
    source = jnp.concatenate([pred_pos, pred_vel, acc_old, jerk_old, jnp.zeros((4, stars), F32)], 0)

    def pick(pick_acc):
        pltpu.matmul_push_rhs(picked, staging_register=0, mxu_index=0)
        for n, piece in enumerate(split3(source)):
            pltpu.matmul_acc_lhs(pick_acc, piece, load_staged_rhs=0 if n == 0 else None)
        own_ref[...] = pltpu.matmul_pop(pick_acc)[:, :slots]

    pl.run_scoped(pick, pltpu.ACC(0)((16, 256), F32))
    own = own_ref[...]
    lane_x = lax.broadcasted_iota(jnp.int32, (8, group), 1) // slots
    state = jnp.concatenate([own[0:6], jnp.zeros((2, slots), F32)], axis=0)
    sink_ref[me] = jnp.where(lane_x == my_x, jnp.concatenate([state] * xs, axis=1), 0.0)

    def star_weights(block, buffer):
        state = star_ref[block]
        mass = state[6:7]
        mass_pos = mass * state[0:3]
        mass_vel = mass * state[3:6]
        empty3 = jnp.zeros((3, stars), F32)
        empty9 = jnp.zeros((9, stars), F32)
        plain_ref[buffer, :32, :] = stack_pieces(
            [*split3(mass_pos), *split3(mass_vel), *split3(mass), empty3], 32
        )
        cross_ref[buffer, :32, :] = stack_pieces(
            [empty9, *split3(-3.0 * mass_pos), empty3, *split3(3.0 * mass)], 32
        )

    star_weights(home, 0)

    pl.semaphore_wait(barrier, 2 * (side - 1) + len(peer_steps))

    def sink_copy(step):
        return pltpu.make_async_remote_copy(
            src_ref=sink_ref.at[me], dst_ref=sink_ref.at[me],
            send_sem=sink_send, recv_sem=sink_recv,
            device_id=peer_id(step), device_id_type=MESH,
        )

    def part_copy(step):
        return pltpu.make_async_remote_copy(
            src_ref=part_ref.at[(my_core + step[0]) & 1], dst_ref=sum_ref.at[me],
            send_sem=part_send, recv_sem=part_recv,
            device_id=peer_id(step), device_id_type=MESH,
        )

    def row_copy(block, number, offset):
        return pltpu.make_async_remote_copy(
            src_ref=star_ref.at[block], dst_ref=star_ref.at[block],
            send_sem=row_send, recv_sem=row_recv.at[number],
            device_id=ring_id(offset, 0), device_id_type=MESH,
        )

    def half_copy(block, unit, offset):
        return pltpu.make_async_remote_copy(
            src_ref=star_ref.at[block], dst_ref=star_ref.at[block],
            send_sem=half_send, recv_sem=half_recv.at[unit],
            device_id=ring_id(0, offset), device_id_type=MESH,
        )

    def many(ref, count, send_sem, recv_sem):
        return pltpu.make_async_remote_copy(
            src_ref=ref.at[pl.ds(0, count)], dst_ref=ref.at[pl.ds(0, count)],
            send_sem=send_sem, recv_sem=recv_sem,
            device_id=peer_id((0, 1)), device_id_type=MESH,
        )

    def row_block(n):
        return second * side + ((first + row[n]) & (side - 1))

    def unit_of(offset, part):
        if offset == side // 2:
            return paired + part
        return 4 * (abs(offset) - 1) + 2 * part + (1 if offset < 0 else 0)

    def pass_on(n):
        block = row_block(n)
        for offset in row[1:]:
            seen = -offset if offset != side // 2 else offset
            half_copy(block, unit_of(seen, n // half), offset).start()

    def take_row(n):
        row_copy(row_block(n), n, row[1]).wait_recv()
        pass_on(n)

    def unit_place(unit):
        last = unit >= paired
        distance = (unit >> 2) + 1
        back = jnp.where(last, 0, unit & 1)
        part = jnp.where(last, unit & 1, (unit >> 1) & 1)
        offset = jnp.where(back == 1, -distance, distance)
        return part, (second + offset) & (side - 1)

    def unit_block(part, w, n):
        number = part * half + n
        offset = ((number + 1) >> 1) * (2 * (number & 1) - 1)
        return w * side + ((first + offset) & (side - 1))

    def take_unit(unit):
        many(star_ref, half, half_send, half_recv.at[unit]).wait_recv()

    for step in peer_steps:
        sink_copy(step).start()
    for n in range(1, side):
        seen = -row[n] if row[n] != side // 2 else row[n]
        row_copy(home, row.index(seen), row[n]).start()
    pass_on(0)
    many(sink_ref, peers - 1, sink_send, sink_recv).wait_recv()

    def core_state(core):
        state = sink_ref[core * xs]
        for x in range(1, xs):
            state = state + sink_ref[core * xs + x]
        return state

    for core in range(cores):
        columns = jnp.transpose(core_state(core))
        for c in range(6):
            wide_ref[c, core * group : (core + 1) * group, :] = jnp.broadcast_to(
                columns[:, c : c + 1], (group, 128)
            )

    def compute(*accumulators):
        plain_acc = accumulators[:tiles]
        cross_acc = accumulators[tiles:]

        def pairs(block, buffer, following):
            pltpu.matmul_push_rhs(
                plain_ref[buffer], staging_register=0, mxu_index=0, transpose=True
            )
            pltpu.matmul_push_rhs(
                cross_ref[buffer], staging_register=0, mxu_index=1, transpose=True
            )
            state = star_ref[block]
            if following is not None:
                star_weights(following, 1 - buffer)
            for step in range(tiles):
                rows = slice(step * tile, (step + 1) * tile)
                sinks = [wide_ref[c, rows, :] for c in range(6)]
                sinks = [jnp.concatenate([value] * (stars // 128), axis=1) for value in sinks]
                sep = [state[c : c + 1] - sinks[c] for c in range(3)]
                rel = [state[3 + c : 4 + c] - sinks[3 + c] for c in range(3)]
                radius_sq = sep[0] * sep[0] + (sep[1] * sep[1] + (sep[2] * sep[2] + SOFTENING))
                radial = sep[0] * rel[0] + sep[1] * rel[1] + sep[2] * rel[2]
                inverse = lax.rsqrt(radius_sq)
                inverse_sq = inverse * inverse
                cube = inverse_sq * inverse
                fifth = (cube * inverse_sq) * radial
                load = 0 if step == 0 else None
                high, low = split2(cube)
                pltpu.matmul_acc_lhs(plain_acc[step], high, load_staged_rhs=load)
                pltpu.matmul_acc_lhs(plain_acc[step], low)
                high, low = split2(fifth)
                pltpu.matmul_acc_lhs(cross_acc[step], high, load_staged_rhs=load)
                pltpu.matmul_acc_lhs(cross_acc[step], low)

        def near_block(kind, number, n=0):
            if kind == "row":
                return row_block(number)
            return unit_block(*unit_place(number), n)

        near = [("row", n) for n in range(5)]
        near += [("unit", unit, n) for unit in (0, 1) for n in range(half)]
        near += [("row", n) for n in (5, 6, 7)]
        near += [("unit", unit, n) for unit in (2, 3) for n in range(half)]
        near += [("unit", 4, 0)]
        takes = {
            ("row", 1): [(take_row, 1), (take_row, 2)],
            ("row", 2): [(take_row, 3), (take_row, 4)],
            ("row", 4): [(take_unit, 0)],
            ("unit", 0, 2): [(take_row, 5), (take_row, 6)],
            ("unit", 0, 3): [(take_unit, 1)],
            ("row", 6): [(take_row, 7)],
            ("row", 7): [(take_unit, 2)],
            ("unit", 2, 3): [(take_unit, 3)],
            ("unit", 3, 3): [(take_unit, 4)],
        }
        for position, here in enumerate(near[:-1]):
            for take, number in takes.get(here, ()):
                take(number)
            if position == 1:
                star_weights(near_block(*here), 1)
            following = None if position == 0 else near_block(*near[position + 1])
            pairs(near_block(*here), position & 1, following)

        def one_unit(unit, _):
            @pl.when(unit + 1 < units)
            def _():
                take_unit(unit + 1)

            part, w = unit_place(unit)
            next_part, next_w = unit_place(jnp.minimum(unit + 1, units - 1))
            for n in range(half):
                block = unit_block(part, w, n)
                if n + 1 < half:
                    following = unit_block(part, w, n + 1)
                else:
                    following = unit_block(next_part, next_w, 0)
                pairs(block, n & 1, following)
            return 0

        lax.fori_loop(4, units, one_unit, 0)
        for core in range(cores):
            sums = [
                (pltpu.matmul_pop(plain_acc[t]) + pltpu.matmul_pop(cross_acc[t]))[:, :128]
                for t in range(core * half_tiles, (core + 1) * half_tiles)
            ]
            rows = jnp.transpose(jnp.concatenate(sums, axis=0))
            state = core_state(core)
            pos = state[0:3]
            vel = state[3:6]
            whole = rows[18:19] + rows[19:20] + rows[20:21]
            cross = rows[21:22] + rows[22:23] + rows[23:24]
            new_acc = (rows[0:3] + rows[3:6] + rows[6:9]) - pos * whole
            new_jerk = (rows[9:12] + rows[12:15] + rows[15:18]) - vel * whole + pos * cross
            part_ref[core] = jnp.concatenate(
                [new_acc, new_jerk, jnp.zeros((2, group), F32)], axis=0
            )

    pl.run_scoped(
        compute,
        *[pltpu.ACC(0)((tile, 256), F32) for _ in range(tiles)],
        *[pltpu.ACC(1)((tile, 256), F32) for _ in range(tiles)],
    )
    for step in peer_steps:
        part_copy(step).start()
    sum_ref[me] = part_ref[my_core]
    many(sink_ref, peers - 1, sink_send, sink_recv).wait_send()
    many(star_ref, side - 1, row_send, row_recv.at[0]).wait_send()
    many(star_ref, side * (side - 1), half_send, half_recv.at[0]).wait_send()
    many(sum_ref, peers - 1, part_send, part_recv).wait_recv()

    total = sum_ref[0]
    for k in range(1, peers):
        total = total + sum_ref[k]
    total = jnp.where(lane_x == my_x, total, 0.0)
    rows = total[:, :slots]
    for x in range(1, xs):
        rows = rows + total[:, x * slots : (x + 1) * slots]
    own_rows = own_ref[...]
    is_live = lax.broadcasted_iota(jnp.int32, (1, slots), 1) < count_ref[...]
    out_ref[...] = correct(own_rows[0:6], own_rows[6:9], own_rows[9:12], rows, is_live)
    many(sum_ref, peers - 1, part_send, part_recv).wait_send()


def solution(mesh):
    teams = mesh.shape["team"]
    cuts = mesh.shape["cuts"]
    xs = 4
    cores = 2
    blocks = teams * cuts // (xs * cores)

    def local(position, velocity, accel_old, jerk_old, star_mass, active_index, active_count):
        stars = position.shape[1]
        slots = active_index.shape[0]
        group = xs * slots
        vmem = pl.BlockSpec(memory_space=pltpu.VMEM)
        dma = pltpu.SemaphoreType.DMA
        return pl.pallas_call(
            functools.partial(step_kernel, teams, cuts, xs, slots, stars, cores),
            out_shape=jax.ShapeDtypeStruct((12, slots), F32),
            in_specs=[pl.BlockSpec(memory_space=pl.ANY)] * 7,
            out_specs=vmem,
            scratch_shapes=[
                *[pltpu.VMEM((3, stars), F32) for _ in range(4)],
                pltpu.VMEM((1, stars), F32),
                pltpu.VMEM((1, slots), jnp.int32),
                pltpu.VMEM((1, 1), jnp.int32),
                dma((7,)),
                pltpu.VMEM((16, slots), F32),
                pltpu.VMEM((blocks, 8, stars), F32),
                pltpu.VMEM((xs * cores, 8, group), F32),
                pltpu.VMEM((cores, 8, group), F32),
                pltpu.VMEM((xs * cores, 8, group), F32),
                pltpu.VMEM((2, 256, stars), BF16),
                pltpu.VMEM((2, 256, stars), BF16),
                pltpu.VMEM((6, cores * group, 128), F32),
                dma((teams // cores,)), dma((2 * (cuts // xs - 1),)), dma, dma, dma, dma, dma, dma,
            ],
            compiler_params=pltpu.CompilerParams(collective_id=0, has_side_effects=True),
            name="hermite_step",
        )(
            position, velocity, accel_old, jerk_old,
            star_mass.reshape(1, stars), active_index.reshape(1, slots), active_count.reshape(1, 1),
        )

    column = P(None, ("team", "cuts"))
    line = P(("team", "cuts"))
    return jax.shard_map(
        local, mesh=mesh, in_specs=(column, column, column, column, line, line, line),
        out_specs=column, check_vma=False,
    )
```

```python
import functools

import jax
import jax.numpy as jnp
from jax import lax
from jax.experimental import pallas as pl
from jax.experimental.pallas import tpu as pltpu
from jax.sharding import PartitionSpec as P

STEP_DT = 0.5
SOFTENING = 0.0004
MESH = pl.DeviceIdType.MESH
F32 = jnp.float32
BF16 = jnp.bfloat16


def split2(value):
    high = value.astype(BF16)
    return high, (value - high.astype(F32)).astype(BF16)


def split3(value):
    high = value.astype(BF16)
    rest = value - high.astype(F32)
    middle = rest.astype(BF16)
    return high, middle, (rest - middle.astype(F32)).astype(BF16)


def stack_pieces(rows, height):
    filled = sum(row.shape[0] for row in rows)
    rows = [row.astype(F32) for row in rows]
    rows = rows + [jnp.zeros((height - filled, rows[0].shape[1]), F32)]
    return jnp.concatenate(rows, axis=0).astype(BF16)


def predict(position, velocity, accel_old, jerk_old):
    pred_pos = position + STEP_DT * (
        velocity + STEP_DT * (accel_old * 0.5 + STEP_DT * (jerk_old * (1.0 / 6.0)))
    )
    pred_vel = velocity + STEP_DT * (accel_old + STEP_DT * (jerk_old * 0.5))
    return (pred_pos, pred_vel)


def correct(sink_state, old_acc, old_jerk, new_rows, is_live):
    pred_pos = sink_state[:3]
    pred_vel = sink_state[3:6]
    new_acc = new_rows[:3]
    new_jerk = new_rows[3:6]
    change = old_acc - new_acc
    second = -6.0 * change - STEP_DT * (4.0 * old_jerk + 2.0 * new_jerk)
    third = 12.0 * change + 6.0 * STEP_DT * (old_jerk + new_jerk)
    new_pos = pred_pos + STEP_DT * STEP_DT * (second * (1.0 / 24.0) + third * (1.0 / 120.0))
    new_vel = pred_vel + STEP_DT * (second * (1.0 / 6.0) + third * (1.0 / 24.0))
    stacked = jnp.concatenate([new_pos, new_vel, new_acc, new_jerk], axis=0)
    return jnp.where(is_live, stacked, 0.0)


def step_kernel(
    teams, cuts, xs, slots, stars, cores,
    pos_hbm, vel_hbm, acc_hbm, jerk_hbm, mass_hbm, index_hbm, count_hbm, out_ref,
    pos_ref, vel_ref, acc_ref, jerk_ref, mass_ref, index_ref, count_ref, load_sem,
    own_ref, star_ref, sink_ref, part_ref, sum_ref, plain_ref, cross_ref, wide_ref,
    row_recv, half_recv, row_send, half_send, sink_send, sink_recv, part_send, part_recv,
):
    team = lax.axis_index("team")
    cut = lax.axis_index("cuts")
    side = teams // cores
    my_y = team >> 1
    my_core = team & 1
    my_z = cut >> 2
    my_x = cut & 3
    first = jnp.where(my_core == 0, my_y, my_z)
    second = jnp.where(my_core == 0, my_z, my_y)
    group = xs * slots
    peers = cores * xs
    tile = 16
    half_tiles = group // tile
    tiles = cores * half_tiles
    me = my_core * xs + my_x
    half = side // 2
    units = 2 * (side - 1)
    paired = units - 2

    peer_steps = [(dc, dx) for dc in range(cores) for dx in range(xs)][1:]

    def peer_id(step):
        dc, dx = step
        return (my_y * cores + ((my_core + dc) & 1), my_z * xs + ((my_x + dx) & 3))

    def ring_id(d_first, d_second):
        u = (first + d_first) & (side - 1)
        w = (second + d_second) & (side - 1)
        y = jnp.where(my_core == 0, u, w)
        z = jnp.where(my_core == 0, w, u)
        return (y * cores + my_core, z * xs + my_x)

    row = [(n + 1) // 2 * (1 if n & 1 else -1) for n in range(side)]
    barrier = pltpu.get_barrier_semaphore()
    for offset in row[1:]:
        pl.semaphore_signal(barrier, inc=1, device_id=ring_id(offset, 0), device_id_type=MESH)
        pl.semaphore_signal(barrier, inc=1, device_id=ring_id(0, offset), device_id_type=MESH)
    for step in peer_steps:
        pl.semaphore_signal(barrier, inc=1, device_id=peer_id(step), device_id_type=MESH)

    loads = [
        pltpu.make_async_copy(source, target, load_sem.at[n])
        for n, (source, target) in enumerate((
            (pos_hbm, pos_ref), (vel_hbm, vel_ref), (acc_hbm, acc_ref), (jerk_hbm, jerk_ref),
            (mass_hbm, mass_ref), (index_hbm, index_ref), (count_hbm, count_ref),
        ))
    ]
    for load in loads:
        load.start()
    plain_ref[...] = jnp.zeros_like(plain_ref)
    cross_ref[...] = jnp.zeros_like(cross_ref)
    for load in loads:
        load.wait()

    acc_old = acc_ref[...]
    jerk_old = jerk_ref[...]
    pred_pos, pred_vel = predict(pos_ref[...], vel_ref[...], acc_old, jerk_old)
    weight = mass_ref[...] * (1.0 / (stars * teams * cuts))
    home = second * side + first
    star_ref[home] = jnp.concatenate(
        [pred_pos, pred_vel, weight, jnp.zeros((1, stars), F32)], axis=0
    )
    index = jnp.concatenate(
        [index_ref[...], jnp.full((1, 256 - slots), -1, jnp.int32)], axis=1
    )
    picked = (
        lax.broadcasted_iota(jnp.int32, (stars, 256), 0) == index
    ).astype(F32).astype(BF16)
    source = jnp.concatenate([pred_pos, pred_vel, acc_old, jerk_old, jnp.zeros((4, stars), F32)], 0)

    def pick(pick_acc):
        pltpu.matmul_push_rhs(picked, staging_register=0, mxu_index=0)
        for n, piece in enumerate(split3(source)):
            pltpu.matmul_acc_lhs(pick_acc, piece, load_staged_rhs=0 if n == 0 else None)
        own_ref[...] = pltpu.matmul_pop(pick_acc)[:, :slots]

    pl.run_scoped(pick, pltpu.ACC(0)((16, 256), F32))
    own = own_ref[...]
    lane_x = lax.broadcasted_iota(jnp.int32, (8, group), 1) // slots
    state = jnp.concatenate([own[0:6], jnp.zeros((2, slots), F32)], axis=0)
    sink_ref[me] = jnp.where(lane_x == my_x, jnp.concatenate([state] * xs, axis=1), 0.0)

    def star_weights(block, buffer):
        state = star_ref[block]
        mass = state[6:7]
        mass_pos = mass * state[0:3]
        mass_vel = mass * state[3:6]
        empty3 = jnp.zeros((3, stars), F32)
        empty9 = jnp.zeros((9, stars), F32)
        plain_ref[buffer, :32, :] = stack_pieces(
            [*split3(mass_pos), *split3(mass_vel), *split3(mass), empty3], 32
        )
        cross_ref[buffer, :32, :] = stack_pieces(
            [empty9, *split3(-3.0 * mass_pos), empty3, *split3(3.0 * mass)], 32
        )

    star_weights(home, 0)

    pl.semaphore_wait(barrier, 2 * (side - 1) + len(peer_steps))

    def sink_copy(step):
        return pltpu.make_async_remote_copy(
            src_ref=sink_ref.at[me], dst_ref=sink_ref.at[me],
            send_sem=sink_send, recv_sem=sink_recv,
            device_id=peer_id(step), device_id_type=MESH,
        )

    def part_copy(step):
        return pltpu.make_async_remote_copy(
            src_ref=part_ref.at[(my_core + step[0]) & 1], dst_ref=sum_ref.at[me],
            send_sem=part_send, recv_sem=part_recv,
            device_id=peer_id(step), device_id_type=MESH,
        )

    def row_copy(block, number, offset):
        return pltpu.make_async_remote_copy(
            src_ref=star_ref.at[block], dst_ref=star_ref.at[block],
            send_sem=row_send, recv_sem=row_recv.at[number],
            device_id=ring_id(offset, 0), device_id_type=MESH,
        )

    def half_copy(block, unit, offset):
        return pltpu.make_async_remote_copy(
            src_ref=star_ref.at[block], dst_ref=star_ref.at[block],
            send_sem=half_send, recv_sem=half_recv.at[unit],
            device_id=ring_id(0, offset), device_id_type=MESH,
        )

    def many(ref, count, send_sem, recv_sem):
        return pltpu.make_async_remote_copy(
            src_ref=ref.at[pl.ds(0, count)], dst_ref=ref.at[pl.ds(0, count)],
            send_sem=send_sem, recv_sem=recv_sem,
            device_id=peer_id((0, 1)), device_id_type=MESH,
        )

    def row_block(n):
        return second * side + ((first + row[n]) & (side - 1))

    def unit_of(offset, part):
        if offset == side // 2:
            return paired + part
        return 4 * (abs(offset) - 1) + 2 * part + (1 if offset < 0 else 0)

    def pass_on(n):
        block = row_block(n)
        for offset in row[1:]:
            seen = -offset if offset != side // 2 else offset
            half_copy(block, unit_of(seen, n // half), offset).start()

    def take_row(n):
        row_copy(row_block(n), n, row[1]).wait_recv()
        pass_on(n)

    def unit_place(unit):
        last = unit >= paired
        distance = (unit >> 2) + 1
        back = jnp.where(last, 0, unit & 1)
        part = jnp.where(last, unit & 1, (unit >> 1) & 1)
        offset = jnp.where(back == 1, -distance, distance)
        return part, (second + offset) & (side - 1)

    def unit_block(part, w, n):
        number = part * half + n
        offset = ((number + 1) >> 1) * (2 * (number & 1) - 1)
        return w * side + ((first + offset) & (side - 1))

    def take_unit(unit):
        many(star_ref, half, half_send, half_recv.at[unit]).wait_recv()

    for step in peer_steps:
        sink_copy(step).start()
    for n in range(1, side):
        seen = -row[n] if row[n] != side // 2 else row[n]
        row_copy(home, row.index(seen), row[n]).start()
    pass_on(0)
    many(sink_ref, peers - 1, sink_send, sink_recv).wait_recv()

    def core_state(core):
        state = sink_ref[core * xs]
        for x in range(1, xs):
            state = state + sink_ref[core * xs + x]
        return state

    for core in range(cores):
        columns = jnp.transpose(core_state(core))
        for c in range(6):
            wide_ref[c, core * group : (core + 1) * group, :] = jnp.broadcast_to(
                columns[:, c : c + 1], (group, 128)
            )

    def compute(*accumulators):
        plain_acc = accumulators[:tiles]
        cross_acc = accumulators[tiles:]

        def pairs(block, buffer, following):
            pltpu.matmul_push_rhs(
                plain_ref[buffer], staging_register=0, mxu_index=0, transpose=True
            )
            pltpu.matmul_push_rhs(
                cross_ref[buffer], staging_register=0, mxu_index=1, transpose=True
            )
            state = star_ref[block]
            star_weights(following, 1 - buffer)
            for step in range(tiles):
                rows = slice(step * tile, (step + 1) * tile)
                sinks = [wide_ref[c, rows, :] for c in range(6)]
                sinks = [jnp.concatenate([value] * (stars // 128), axis=1) for value in sinks]
                sep = [state[c : c + 1] - sinks[c] for c in range(3)]
                rel = [state[3 + c : 4 + c] - sinks[3 + c] for c in range(3)]
                radius_sq = sep[0] * sep[0] + (sep[1] * sep[1] + (sep[2] * sep[2] + SOFTENING))
                radial = sep[0] * rel[0] + sep[1] * rel[1] + sep[2] * rel[2]
                inverse = lax.rsqrt(radius_sq)
                inverse_sq = inverse * inverse
                cube = inverse_sq * inverse
                fifth = (cube * inverse_sq) * radial
                load = 0 if step == 0 else None
                high, low = split2(cube)
                pltpu.matmul_acc_lhs(plain_acc[step], high, load_staged_rhs=load)
                pltpu.matmul_acc_lhs(plain_acc[step], low)
                high, low = split2(fifth)
                pltpu.matmul_acc_lhs(cross_acc[step], high, load_staged_rhs=load)
                pltpu.matmul_acc_lhs(cross_acc[step], low)

        def near_block(kind, number, n=0):
            if kind == "row":
                return row_block(number)
            return unit_block(*unit_place(number), n)

        near = [("row", n) for n in range(side)] + [("unit", 0, 0)]
        takes = {
            ("row", 0): [(take_row, 1), (take_row, 2)],
            ("row", 1): [(take_row, 3), (take_row, 4)],
            ("row", 3): [(take_row, 5), (take_row, 6)],
            ("row", 5): [(take_row, 7)],
            ("row", 7): [(take_unit, 0)],
        }
        for position, here in enumerate(near[:-1]):
            for take, number in takes.get(here, ()):
                take(number)
            pairs(near_block(*here), position & 1, near_block(*near[position + 1]))

        def one_unit(unit, _):
            @pl.when(unit + 1 < units)
            def _():
                take_unit(unit + 1)

            part, w = unit_place(unit)
            next_part, next_w = unit_place(jnp.minimum(unit + 1, units - 1))
            for n in range(half):
                block = unit_block(part, w, n)
                if n + 1 < half:
                    following = unit_block(part, w, n + 1)
                else:
                    following = unit_block(next_part, next_w, 0)
                pairs(block, n & 1, following)
            return 0

        lax.fori_loop(0, units, one_unit, 0)
        for core in range(cores):
            sums = [
                (pltpu.matmul_pop(plain_acc[t]) + pltpu.matmul_pop(cross_acc[t]))[:, :128]
                for t in range(core * half_tiles, (core + 1) * half_tiles)
            ]
            rows = jnp.transpose(jnp.concatenate(sums, axis=0))
            state = core_state(core)
            pos = state[0:3]
            vel = state[3:6]
            whole = rows[18:19] + rows[19:20] + rows[20:21]
            cross = rows[21:22] + rows[22:23] + rows[23:24]
            new_acc = (rows[0:3] + rows[3:6] + rows[6:9]) - pos * whole
            new_jerk = (rows[9:12] + rows[12:15] + rows[15:18]) - vel * whole + pos * cross
            part_ref[core] = jnp.concatenate(
                [new_acc, new_jerk, jnp.zeros((2, group), F32)], axis=0
            )

    pl.run_scoped(
        compute,
        *[pltpu.ACC(0)((tile, 256), F32) for _ in range(tiles)],
        *[pltpu.ACC(1)((tile, 256), F32) for _ in range(tiles)],
    )
    for step in peer_steps:
        part_copy(step).start()
    sum_ref[me] = part_ref[my_core]
    many(sink_ref, peers - 1, sink_send, sink_recv).wait_send()
    many(star_ref, side - 1, row_send, row_recv.at[0]).wait_send()
    many(star_ref, side * (side - 1), half_send, half_recv.at[0]).wait_send()
    many(sum_ref, peers - 1, part_send, part_recv).wait_recv()

    total = sum_ref[0]
    for k in range(1, peers):
        total = total + sum_ref[k]
    total = jnp.where(lane_x == my_x, total, 0.0)
    rows = total[:, :slots]
    for x in range(1, xs):
        rows = rows + total[:, x * slots : (x + 1) * slots]
    own_rows = own_ref[...]
    is_live = lax.broadcasted_iota(jnp.int32, (1, slots), 1) < count_ref[...]
    out_ref[...] = correct(own_rows[0:6], own_rows[6:9], own_rows[9:12], rows, is_live)
    many(sum_ref, peers - 1, part_send, part_recv).wait_send()


def solution(mesh):
    teams = mesh.shape["team"]
    cuts = mesh.shape["cuts"]
    xs = 4
    cores = 2
    blocks = teams * cuts // (xs * cores)

    def local(position, velocity, accel_old, jerk_old, star_mass, active_index, active_count):
        stars = position.shape[1]
        slots = active_index.shape[0]
        group = xs * slots
        vmem = pl.BlockSpec(memory_space=pltpu.VMEM)
        dma = pltpu.SemaphoreType.DMA
        return pl.pallas_call(
            functools.partial(step_kernel, teams, cuts, xs, slots, stars, cores),
            out_shape=jax.ShapeDtypeStruct((12, slots), F32),
            in_specs=[pl.BlockSpec(memory_space=pl.ANY)] * 7,
            out_specs=vmem,
            scratch_shapes=[
                *[pltpu.VMEM((3, stars), F32) for _ in range(4)],
                pltpu.VMEM((1, stars), F32),
                pltpu.VMEM((1, slots), jnp.int32),
                pltpu.VMEM((1, 1), jnp.int32),
                dma((7,)),
                pltpu.VMEM((16, slots), F32),
                pltpu.VMEM((blocks, 8, stars), F32),
                pltpu.VMEM((xs * cores, 8, group), F32),
                pltpu.VMEM((cores, 8, group), F32),
                pltpu.VMEM((xs * cores, 8, group), F32),
                pltpu.VMEM((2, 256, stars), BF16),
                pltpu.VMEM((2, 256, stars), BF16),
                pltpu.VMEM((6, cores * group, 128), F32),
                dma((teams // cores,)), dma((2 * (cuts // xs - 1),)), dma, dma, dma, dma, dma, dma,
            ],
            compiler_params=pltpu.CompilerParams(collective_id=0, has_side_effects=True),
            name="hermite_step",
        )(
            position, velocity, accel_old, jerk_old,
            star_mass.reshape(1, stars), active_index.reshape(1, slots), active_count.reshape(1, 1),
        )

    column = P(None, ("team", "cuts"))
    line = P(("team", "cuts"))
    return jax.shard_map(
        local, mesh=mesh, in_specs=(column, column, column, column, line, line, line),
        out_specs=column, check_vma=False,
    )
```

```python
import functools

import jax
import jax.numpy as jnp
from jax import lax
from jax.experimental import pallas as pl
from jax.experimental.pallas import tpu as pltpu
from jax.sharding import PartitionSpec as P

STEP_DT = 0.5
SOFTENING = 0.0004
MESH = pl.DeviceIdType.MESH
F32 = jnp.float32
BF16 = jnp.bfloat16


def split2(value):
    high = value.astype(BF16)
    return high, (value - high.astype(F32)).astype(BF16)


def split3(value):
    high = value.astype(BF16)
    rest = value - high.astype(F32)
    middle = rest.astype(BF16)
    return high, middle, (rest - middle.astype(F32)).astype(BF16)


def stack_pieces(rows, height):
    filled = sum(row.shape[0] for row in rows)
    rows = [row.astype(F32) for row in rows]
    rows = rows + [jnp.zeros((height - filled, rows[0].shape[1]), F32)]
    return jnp.concatenate(rows, axis=0).astype(BF16)


def predict(position, velocity, accel_old, jerk_old):
    pred_pos = position + STEP_DT * (
        velocity + STEP_DT * (accel_old * 0.5 + STEP_DT * (jerk_old * (1.0 / 6.0)))
    )
    pred_vel = velocity + STEP_DT * (accel_old + STEP_DT * (jerk_old * 0.5))
    return (pred_pos, pred_vel)


def correct(sink_state, old_acc, old_jerk, new_rows, is_live):
    pred_pos = sink_state[:3]
    pred_vel = sink_state[3:6]
    new_acc = new_rows[:3]
    new_jerk = new_rows[3:6]
    change = old_acc - new_acc
    second = -6.0 * change - STEP_DT * (4.0 * old_jerk + 2.0 * new_jerk)
    third = 12.0 * change + 6.0 * STEP_DT * (old_jerk + new_jerk)
    new_pos = pred_pos + STEP_DT * STEP_DT * (second * (1.0 / 24.0) + third * (1.0 / 120.0))
    new_vel = pred_vel + STEP_DT * (second * (1.0 / 6.0) + third * (1.0 / 24.0))
    stacked = jnp.concatenate([new_pos, new_vel, new_acc, new_jerk], axis=0)
    return jnp.where(is_live, stacked, 0.0)


def step_kernel(
    teams, cuts, xs, slots, stars, cores,
    pos_hbm, vel_hbm, acc_hbm, jerk_hbm, mass_hbm, index_hbm, count_hbm, out_ref,
    pos_ref, vel_ref, acc_ref, jerk_ref, mass_ref, index_ref, count_ref, load_sem,
    own_ref, star_ref, sink_ref, part_ref, sum_ref, plain_ref, cross_ref, wide_ref,
    row_recv, half_recv, row_send, half_send, sink_send, sink_recv, part_send, part_recv,
):
    team = lax.axis_index("team")
    cut = lax.axis_index("cuts")
    side = teams // cores
    my_y = team >> 1
    my_core = team & 1
    my_z = cut >> 2
    my_x = cut & 3
    first = jnp.where(my_core == 0, my_y, my_z)
    second = jnp.where(my_core == 0, my_z, my_y)
    group = xs * slots
    peers = cores * xs
    tile = 16
    half_tiles = group // tile
    tiles = cores * half_tiles
    me = my_core * xs + my_x
    half = side // 2
    units = 2 * (side - 1)
    paired = units - 2

    peer_steps = [(dc, dx) for dc in range(cores) for dx in range(xs)][1:]

    def peer_id(step):
        dc, dx = step
        return (my_y * cores + ((my_core + dc) & 1), my_z * xs + ((my_x + dx) & 3))

    def ring_id(d_first, d_second):
        u = (first + d_first) & (side - 1)
        w = (second + d_second) & (side - 1)
        y = jnp.where(my_core == 0, u, w)
        z = jnp.where(my_core == 0, w, u)
        return (y * cores + my_core, z * xs + my_x)

    row = [(n + 1) // 2 * (1 if n & 1 else -1) for n in range(side)]
    barrier = pltpu.get_barrier_semaphore()
    for offset in row[1:]:
        pl.semaphore_signal(barrier, inc=1, device_id=ring_id(offset, 0), device_id_type=MESH)
        pl.semaphore_signal(barrier, inc=1, device_id=ring_id(0, offset), device_id_type=MESH)
    for step in peer_steps:
        pl.semaphore_signal(barrier, inc=1, device_id=peer_id(step), device_id_type=MESH)

    loads = [
        pltpu.make_async_copy(source, target, load_sem.at[n])
        for n, (source, target) in enumerate((
            (pos_hbm, pos_ref), (vel_hbm, vel_ref), (acc_hbm, acc_ref), (jerk_hbm, jerk_ref),
            (mass_hbm, mass_ref), (index_hbm, index_ref), (count_hbm, count_ref),
        ))
    ]
    for load in loads:
        load.start()
    plain_ref[...] = jnp.zeros_like(plain_ref)
    cross_ref[...] = jnp.zeros_like(cross_ref)
    for load in loads:
        load.wait()

    acc_old = acc_ref[...]
    jerk_old = jerk_ref[...]
    pred_pos, pred_vel = predict(pos_ref[...], vel_ref[...], acc_old, jerk_old)
    weight = mass_ref[...] * (1.0 / (stars * teams * cuts))
    home = second * side + first
    star_ref[home] = jnp.concatenate(
        [pred_pos, pred_vel, weight, jnp.zeros((1, stars), F32)], axis=0
    )
    index = jnp.concatenate(
        [index_ref[...], jnp.full((1, 256 - slots), -1, jnp.int32)], axis=1
    )
    picked = (
        lax.broadcasted_iota(jnp.int32, (stars, 256), 0) == index
    ).astype(F32).astype(BF16)
    source = jnp.concatenate([pred_pos, pred_vel, acc_old, jerk_old, jnp.zeros((4, stars), F32)], 0)

    def pick(pick_acc):
        pltpu.matmul_push_rhs(picked, staging_register=0, mxu_index=0)
        for n, piece in enumerate(split3(source)):
            pltpu.matmul_acc_lhs(pick_acc, piece, load_staged_rhs=0 if n == 0 else None)
        own_ref[...] = pltpu.matmul_pop(pick_acc)[:, :slots]

    pl.run_scoped(pick, pltpu.ACC(0)((16, 256), F32))
    own = own_ref[...]
    lane_x = lax.broadcasted_iota(jnp.int32, (8, group), 1) // slots
    state = jnp.concatenate([own[0:6], jnp.zeros((2, slots), F32)], axis=0)
    sink_ref[me] = jnp.where(lane_x == my_x, jnp.concatenate([state] * xs, axis=1), 0.0)

    def star_weights(block, buffer):
        state = star_ref[block]
        mass = state[6:7]
        mass_pos = mass * state[0:3]
        mass_vel = mass * state[3:6]
        empty3 = jnp.zeros((3, stars), F32)
        empty9 = jnp.zeros((9, stars), F32)
        plain_ref[buffer, :32, :] = stack_pieces(
            [*split3(mass_pos), *split3(mass_vel), *split3(mass), empty3], 32
        )
        cross_ref[buffer, :32, :] = stack_pieces(
            [empty9, *split3(-3.0 * mass_pos), empty3, *split3(3.0 * mass)], 32
        )

    star_weights(home, 0)

    pl.semaphore_wait(barrier, 2 * (side - 1) + len(peer_steps))

    def sink_copy(step):
        return pltpu.make_async_remote_copy(
            src_ref=sink_ref.at[me], dst_ref=sink_ref.at[me],
            send_sem=sink_send, recv_sem=sink_recv,
            device_id=peer_id(step), device_id_type=MESH,
        )

    def part_copy(step):
        return pltpu.make_async_remote_copy(
            src_ref=part_ref.at[(my_core + step[0]) & 1], dst_ref=sum_ref.at[me],
            send_sem=part_send, recv_sem=part_recv,
            device_id=peer_id(step), device_id_type=MESH,
        )

    def row_copy(block, number, offset):
        return pltpu.make_async_remote_copy(
            src_ref=star_ref.at[block], dst_ref=star_ref.at[block],
            send_sem=row_send, recv_sem=row_recv.at[number],
            device_id=ring_id(offset, 0), device_id_type=MESH,
        )

    def half_copy(block, unit, offset):
        return pltpu.make_async_remote_copy(
            src_ref=star_ref.at[block], dst_ref=star_ref.at[block],
            send_sem=half_send, recv_sem=half_recv.at[unit],
            device_id=ring_id(0, offset), device_id_type=MESH,
        )

    def many(ref, count, send_sem, recv_sem):
        return pltpu.make_async_remote_copy(
            src_ref=ref.at[pl.ds(0, count)], dst_ref=ref.at[pl.ds(0, count)],
            send_sem=send_sem, recv_sem=recv_sem,
            device_id=peer_id((0, 1)), device_id_type=MESH,
        )

    def row_block(n):
        return second * side + ((first + row[n]) & (side - 1))

    def unit_of(offset, part):
        if offset == side // 2:
            return paired + part
        return 4 * (abs(offset) - 1) + 2 * part + (1 if offset < 0 else 0)

    def pass_on(n):
        block = row_block(n)
        for offset in row[1:]:
            seen = -offset if offset != side // 2 else offset
            half_copy(block, unit_of(seen, n // half), offset).start()

    def take_row(n):
        row_copy(row_block(n), n, row[1]).wait_recv()
        pass_on(n)

    def unit_place(unit):
        last = unit >= paired
        distance = (unit >> 2) + 1
        back = jnp.where(last, 0, unit & 1)
        part = jnp.where(last, unit & 1, (unit >> 1) & 1)
        offset = jnp.where(back == 1, -distance, distance)
        return part, (second + offset) & (side - 1)

    def unit_block(part, w, n):
        number = part * half + n
        offset = ((number + 1) >> 1) * (2 * (number & 1) - 1)
        return w * side + ((first + offset) & (side - 1))

    def take_unit(unit):
        many(star_ref, half, half_send, half_recv.at[unit]).wait_recv()

    for step in peer_steps:
        sink_copy(step).start()
    for n in range(1, side):
        seen = -row[n] if row[n] != side // 2 else row[n]
        row_copy(home, row.index(seen), row[n]).start()
    pass_on(0)
    many(sink_ref, peers - 1, sink_send, sink_recv).wait_recv()

    def core_state(core):
        state = sink_ref[core * xs]
        for x in range(1, xs):
            state = state + sink_ref[core * xs + x]
        return state

    for core in range(cores):
        columns = jnp.transpose(core_state(core))
        for c in range(6):
            wide_ref[c, core * group : (core + 1) * group, :] = jnp.broadcast_to(
                columns[:, c : c + 1], (group, 128)
            )

    def compute(*accumulators):
        plain_acc = accumulators[:tiles]
        cross_acc = accumulators[tiles:]

        def pairs(block, buffer, following):
            pltpu.matmul_push_rhs(
                plain_ref[buffer], staging_register=0, mxu_index=0, transpose=True
            )
            pltpu.matmul_push_rhs(
                cross_ref[buffer], staging_register=0, mxu_index=1, transpose=True
            )
            state = star_ref[block]
            if following is not None:
                star_weights(following, 1 - buffer)
            for step in range(tiles):
                rows = slice(step * tile, (step + 1) * tile)
                sinks = [wide_ref[c, rows, :] for c in range(6)]
                sinks = [jnp.concatenate([value] * (stars // 128), axis=1) for value in sinks]
                sep = [state[c : c + 1] - sinks[c] for c in range(3)]
                rel = [state[3 + c : 4 + c] - sinks[3 + c] for c in range(3)]
                radius_sq = sep[0] * sep[0] + (sep[1] * sep[1] + (sep[2] * sep[2] + SOFTENING))
                radial = sep[0] * rel[0] + sep[1] * rel[1] + sep[2] * rel[2]
                inverse = lax.rsqrt(radius_sq)
                inverse_sq = inverse * inverse
                cube = inverse_sq * inverse
                fifth = (cube * inverse_sq) * radial
                load = 0 if step == 0 else None
                high, low = split2(cube)
                pltpu.matmul_acc_lhs(plain_acc[step], high, load_staged_rhs=load)
                pltpu.matmul_acc_lhs(plain_acc[step], low)
                high, low = split2(fifth)
                pltpu.matmul_acc_lhs(cross_acc[step], high, load_staged_rhs=load)
                pltpu.matmul_acc_lhs(cross_acc[step], low)

        def near_block(kind, number, n=0):
            if kind == "row":
                return row_block(number)
            return unit_block(*unit_place(number), n)

        near = [("row", n) for n in range(side)] + [("unit", 0, 0)]
        takes = {
            ("row", 0): [(take_row, 1), (take_row, 2)],
            ("row", 2): [(take_row, 3), (take_row, 4)],
            ("row", 4): [(take_row, 5), (take_row, 6)],
            ("row", 6): [(take_row, 7)],
            ("row", 7): [(take_unit, 0)],
        }
        for position, here in enumerate(near[:-1]):
            for take, number in takes.get(here, ()):
                take(number)
            pairs(near_block(*here), position & 1, near_block(*near[position + 1]))

        def one_unit(unit, last=False):
            part, w = unit_place(unit)
            for n in range(half):
                if n + 1 < half:
                    following = unit_block(part, w, n + 1)
                elif last:
                    following = None
                else:
                    take_unit(unit + 1)
                    following = unit_block(*unit_place(unit + 1), 0)
                pairs(unit_block(part, w, n), n & 1, following)

        def next_unit(unit, _):
            one_unit(unit)
            return 0

        lax.fori_loop(0, units - 1, next_unit, 0)
        one_unit(jnp.int32(units - 1), last=True)
        for core in range(cores):
            sums = [
                (pltpu.matmul_pop(plain_acc[t]) + pltpu.matmul_pop(cross_acc[t]))[:, :128]
                for t in range(core * half_tiles, (core + 1) * half_tiles)
            ]
            rows = jnp.transpose(jnp.concatenate(sums, axis=0))
            state = core_state(core)
            pos = state[0:3]
            vel = state[3:6]
            whole = rows[18:19] + rows[19:20] + rows[20:21]
            cross = rows[21:22] + rows[22:23] + rows[23:24]
            new_acc = (rows[0:3] + rows[3:6] + rows[6:9]) - pos * whole
            new_jerk = (rows[9:12] + rows[12:15] + rows[15:18]) - vel * whole + pos * cross
            part_ref[core] = jnp.concatenate(
                [new_acc, new_jerk, jnp.zeros((2, group), F32)], axis=0
            )

    pl.run_scoped(
        compute,
        *[pltpu.ACC(0)((tile, 256), F32) for _ in range(tiles)],
        *[pltpu.ACC(1)((tile, 256), F32) for _ in range(tiles)],
    )
    for step in peer_steps:
        part_copy(step).start()
    sum_ref[me] = part_ref[my_core]
    many(sink_ref, peers - 1, sink_send, sink_recv).wait_send()
    many(star_ref, side - 1, row_send, row_recv.at[0]).wait_send()
    many(star_ref, side * (side - 1), half_send, half_recv.at[0]).wait_send()
    many(sum_ref, peers - 1, part_send, part_recv).wait_recv()

    total = sum_ref[0]
    for k in range(1, peers):
        total = total + sum_ref[k]
    total = jnp.where(lane_x == my_x, total, 0.0)
    rows = total[:, :slots]
    for x in range(1, xs):
        rows = rows + total[:, x * slots : (x + 1) * slots]
    own_rows = own_ref[...]
    is_live = lax.broadcasted_iota(jnp.int32, (1, slots), 1) < count_ref[...]
    out_ref[...] = correct(own_rows[0:6], own_rows[6:9], own_rows[9:12], rows, is_live)
    many(sum_ref, peers - 1, part_send, part_recv).wait_send()


def solution(mesh):
    teams = mesh.shape["team"]
    cuts = mesh.shape["cuts"]
    xs = 4
    cores = 2
    blocks = teams * cuts // (xs * cores)

    def local(position, velocity, accel_old, jerk_old, star_mass, active_index, active_count):
        stars = position.shape[1]
        slots = active_index.shape[0]
        group = xs * slots
        vmem = pl.BlockSpec(memory_space=pltpu.VMEM)
        dma = pltpu.SemaphoreType.DMA
        return pl.pallas_call(
            functools.partial(step_kernel, teams, cuts, xs, slots, stars, cores),
            out_shape=jax.ShapeDtypeStruct((12, slots), F32),
            in_specs=[pl.BlockSpec(memory_space=pl.ANY)] * 7,
            out_specs=vmem,
            scratch_shapes=[
                *[pltpu.VMEM((3, stars), F32) for _ in range(4)],
                pltpu.VMEM((1, stars), F32),
                pltpu.VMEM((1, slots), jnp.int32),
                pltpu.VMEM((1, 1), jnp.int32),
                dma((7,)),
                pltpu.VMEM((16, slots), F32),
                pltpu.VMEM((blocks, 8, stars), F32),
                pltpu.VMEM((xs * cores, 8, group), F32),
                pltpu.VMEM((cores, 8, group), F32),
                pltpu.VMEM((xs * cores, 8, group), F32),
                pltpu.VMEM((2, 256, stars), BF16),
                pltpu.VMEM((2, 256, stars), BF16),
                pltpu.VMEM((6, cores * group, 128), F32),
                dma((teams // cores,)), dma((2 * (cuts // xs - 1),)), dma, dma, dma, dma, dma, dma,
            ],
            compiler_params=pltpu.CompilerParams(collective_id=0, has_side_effects=True),
            name="hermite_step",
        )(
            position, velocity, accel_old, jerk_old,
            star_mass.reshape(1, stars), active_index.reshape(1, slots), active_count.reshape(1, 1),
        )

    column = P(None, ("team", "cuts"))
    line = P(("team", "cuts"))
    return jax.shard_map(
        local, mesh=mesh, in_specs=(column, column, column, column, line, line, line),
        out_specs=column, check_vma=False,
    )
```

```python
import functools

import jax
import jax.numpy as jnp
from jax import lax
from jax.experimental import pallas as pl
from jax.experimental.pallas import tpu as pltpu
from jax.sharding import PartitionSpec as P

STEP_DT = 0.5
SOFTENING = 0.0004
MESH = pl.DeviceIdType.MESH
F32 = jnp.float32
BF16 = jnp.bfloat16


def split2(value):
    high = value.astype(BF16)
    return high, (value - high.astype(F32)).astype(BF16)


def split3(value):
    high = value.astype(BF16)
    rest = value - high.astype(F32)
    middle = rest.astype(BF16)
    return high, middle, (rest - middle.astype(F32)).astype(BF16)


def stack_pieces(rows, height):
    filled = sum(row.shape[0] for row in rows)
    rows = [row.astype(F32) for row in rows]
    rows = rows + [jnp.zeros((height - filled, rows[0].shape[1]), F32)]
    return jnp.concatenate(rows, axis=0).astype(BF16)


def predict(position, velocity, accel_old, jerk_old):
    pred_pos = position + STEP_DT * (
        velocity + STEP_DT * (accel_old * 0.5 + STEP_DT * (jerk_old * (1.0 / 6.0)))
    )
    pred_vel = velocity + STEP_DT * (accel_old + STEP_DT * (jerk_old * 0.5))
    return (pred_pos, pred_vel)


def correct(sink_state, old_acc, old_jerk, new_rows, is_live):
    pred_pos = sink_state[:3]
    pred_vel = sink_state[3:6]
    new_acc = new_rows[:3]
    new_jerk = new_rows[3:6]
    change = old_acc - new_acc
    second = -6.0 * change - STEP_DT * (4.0 * old_jerk + 2.0 * new_jerk)
    third = 12.0 * change + 6.0 * STEP_DT * (old_jerk + new_jerk)
    new_pos = pred_pos + STEP_DT * STEP_DT * (second * (1.0 / 24.0) + third * (1.0 / 120.0))
    new_vel = pred_vel + STEP_DT * (second * (1.0 / 6.0) + third * (1.0 / 24.0))
    stacked = jnp.concatenate([new_pos, new_vel, new_acc, new_jerk], axis=0)
    return jnp.where(is_live, stacked, 0.0)


def step_kernel(
    teams, cuts, xs, slots, stars, cores,
    pos_hbm, vel_hbm, acc_hbm, jerk_hbm, mass_hbm, index_hbm, count_hbm, out_ref,
    pos_ref, vel_ref, acc_ref, jerk_ref, mass_ref, index_ref, count_ref, load_sem,
    own_ref, star_ref, sink_ref, part_ref, sum_ref, plain_ref, cross_ref, wide_ref,
    row_recv, half_recv, row_send, half_send, sink_send, sink_recv, part_send, part_recv,
):
    team = lax.axis_index("team")
    cut = lax.axis_index("cuts")
    side = teams // cores
    my_y = team >> 1
    my_core = team & 1
    my_z = cut >> 2
    my_x = cut & 3
    first = jnp.where(my_core == 0, my_y, my_z)
    second = jnp.where(my_core == 0, my_z, my_y)
    group = xs * slots
    peers = cores * xs
    tile = 16
    half_tiles = group // tile
    tiles = cores * half_tiles
    me = my_core * xs + my_x
    half = side // 2
    units = 2 * (side - 1)
    paired = units - 2

    peer_steps = [(dc, dx) for dx in (2, 1, 3, 0) for dc in range(cores) if dc or dx]

    def peer_id(step):
        dc, dx = step
        return (my_y * cores + ((my_core + dc) & 1), my_z * xs + ((my_x + dx) & 3))

    def ring_id(d_first, d_second):
        u = (first + d_first) & (side - 1)
        w = (second + d_second) & (side - 1)
        y = jnp.where(my_core == 0, u, w)
        z = jnp.where(my_core == 0, w, u)
        return (y * cores + my_core, z * xs + my_x)

    row = [(n + 1) // 2 * (1 if n & 1 else -1) for n in range(side)]
    barrier = pltpu.get_barrier_semaphore()
    for offset in reversed(row[1:]):
        pl.semaphore_signal(barrier, inc=1, device_id=ring_id(offset, 0), device_id_type=MESH)
        pl.semaphore_signal(barrier, inc=1, device_id=ring_id(0, offset), device_id_type=MESH)
    for step in peer_steps:
        pl.semaphore_signal(barrier, inc=1, device_id=peer_id(step), device_id_type=MESH)

    loads = [
        pltpu.make_async_copy(source, target, load_sem.at[n])
        for n, (source, target) in enumerate((
            (pos_hbm, pos_ref), (vel_hbm, vel_ref), (acc_hbm, acc_ref), (jerk_hbm, jerk_ref),
            (mass_hbm, mass_ref), (index_hbm, index_ref), (count_hbm, count_ref),
        ))
    ]
    for load in loads:
        load.start()
    plain_ref[...] = jnp.zeros_like(plain_ref)
    cross_ref[...] = jnp.zeros_like(cross_ref)
    for load in loads:
        load.wait()

    acc_old = acc_ref[...]
    jerk_old = jerk_ref[...]
    pred_pos, pred_vel = predict(pos_ref[...], vel_ref[...], acc_old, jerk_old)
    weight = mass_ref[...] * (1.0 / (stars * teams * cuts))
    home = second * side + first
    star_ref[home] = jnp.concatenate(
        [pred_pos, pred_vel, weight, jnp.zeros((1, stars), F32)], axis=0
    )
    index = jnp.concatenate(
        [index_ref[...], jnp.full((1, 256 - slots), -1, jnp.int32)], axis=1
    )
    picked = (
        lax.broadcasted_iota(jnp.int32, (stars, 256), 0) == index
    ).astype(F32).astype(BF16)
    source = jnp.concatenate([pred_pos, pred_vel, acc_old, jerk_old, jnp.zeros((4, stars), F32)], 0)

    def pick(pick_acc):
        pltpu.matmul_push_rhs(picked, staging_register=0, mxu_index=0)
        for n, piece in enumerate(split3(source)):
            pltpu.matmul_acc_lhs(pick_acc, piece, load_staged_rhs=0 if n == 0 else None)
        own_ref[...] = pltpu.matmul_pop(pick_acc)[:, :slots]

    pl.run_scoped(pick, pltpu.ACC(0)((16, 256), F32))
    own = own_ref[...]
    lane_x = lax.broadcasted_iota(jnp.int32, (8, group), 1) // slots
    state = jnp.concatenate([own[0:6], jnp.zeros((2, slots), F32)], axis=0)
    sink_ref[me] = jnp.where(lane_x == my_x, jnp.concatenate([state] * xs, axis=1), 0.0)

    def star_weights(block, buffer):
        state = star_ref[block]
        mass = state[6:7]
        mass_pos = mass * state[0:3]
        mass_vel = mass * state[3:6]
        empty3 = jnp.zeros((3, stars), F32)
        empty9 = jnp.zeros((9, stars), F32)
        plain_ref[buffer, :32, :] = stack_pieces(
            [*split3(mass_pos), *split3(mass_vel), *split3(mass), empty3], 32
        )
        cross_ref[buffer, :32, :] = stack_pieces(
            [empty9, *split3(-3.0 * mass_pos), empty3, *split3(3.0 * mass)], 32
        )

    star_weights(home, 0)

    pl.semaphore_wait(barrier, 2 * (side - 1) + len(peer_steps))

    def sink_copy(step):
        return pltpu.make_async_remote_copy(
            src_ref=sink_ref.at[me], dst_ref=sink_ref.at[me],
            send_sem=sink_send, recv_sem=sink_recv,
            device_id=peer_id(step), device_id_type=MESH,
        )

    def part_copy(step):
        return pltpu.make_async_remote_copy(
            src_ref=part_ref.at[(my_core + step[0]) & 1], dst_ref=sum_ref.at[me],
            send_sem=part_send, recv_sem=part_recv,
            device_id=peer_id(step), device_id_type=MESH,
        )

    def row_copy(block, number, offset):
        return pltpu.make_async_remote_copy(
            src_ref=star_ref.at[block], dst_ref=star_ref.at[block],
            send_sem=row_send, recv_sem=row_recv.at[number],
            device_id=ring_id(offset, 0), device_id_type=MESH,
        )

    def half_copy(block, unit, offset):
        return pltpu.make_async_remote_copy(
            src_ref=star_ref.at[block], dst_ref=star_ref.at[block],
            send_sem=half_send, recv_sem=half_recv.at[unit],
            device_id=ring_id(0, offset), device_id_type=MESH,
        )

    def many(ref, count, send_sem, recv_sem):
        return pltpu.make_async_remote_copy(
            src_ref=ref.at[pl.ds(0, count)], dst_ref=ref.at[pl.ds(0, count)],
            send_sem=send_sem, recv_sem=recv_sem,
            device_id=peer_id((0, 1)), device_id_type=MESH,
        )

    def row_block(n):
        return second * side + ((first + row[n]) & (side - 1))

    def unit_of(offset, part):
        if offset == side // 2:
            return paired + part
        return 4 * (abs(offset) - 1) + 2 * part + (1 if offset < 0 else 0)

    def pass_on(n):
        block = row_block(n)
        for offset in row[1:]:
            seen = -offset if offset != side // 2 else offset
            half_copy(block, unit_of(seen, n // half), offset).start()

    def take_row(n):
        row_copy(row_block(n), n, row[1]).wait_recv()
        pass_on(n)

    def unit_place(unit):
        last = unit >= paired
        distance = (unit >> 2) + 1
        back = jnp.where(last, 0, unit & 1)
        part = jnp.where(last, unit & 1, (unit >> 1) & 1)
        offset = jnp.where(back == 1, -distance, distance)
        return part, (second + offset) & (side - 1)

    def unit_block(part, w, n):
        number = part * half + n
        offset = ((number + 1) >> 1) * (2 * (number & 1) - 1)
        return w * side + ((first + offset) & (side - 1))

    def take_unit(unit):
        many(star_ref, half, half_send, half_recv.at[unit]).wait_recv()

    for step in peer_steps:
        sink_copy(step).start()
    for n in range(1, side):
        seen = -row[n] if row[n] != side // 2 else row[n]
        row_copy(home, row.index(seen), row[n]).start()
    pass_on(0)
    many(sink_ref, peers - 1, sink_send, sink_recv).wait_recv()

    def core_state(core):
        state = sink_ref[core * xs]
        for x in range(1, xs):
            state = state + sink_ref[core * xs + x]
        return state

    for core in range(cores):
        columns = jnp.transpose(core_state(core))
        for c in range(6):
            wide_ref[c, core * group : (core + 1) * group, :] = jnp.broadcast_to(
                columns[:, c : c + 1], (group, 128)
            )

    def compute(*accumulators):
        plain_acc = accumulators[:tiles]
        cross_acc = accumulators[tiles:]

        def pairs(block, buffer, following):
            pltpu.matmul_push_rhs(
                plain_ref[buffer], staging_register=0, mxu_index=0, transpose=True
            )
            pltpu.matmul_push_rhs(
                cross_ref[buffer], staging_register=0, mxu_index=1, transpose=True
            )
            state = star_ref[block]
            if following is not None:
                star_weights(following, 1 - buffer)
            for step in range(tiles):
                rows = slice(step * tile, (step + 1) * tile)
                sinks = [wide_ref[c, rows, :] for c in range(6)]
                sinks = [jnp.concatenate([value] * (stars // 128), axis=1) for value in sinks]
                sep = [state[c : c + 1] - sinks[c] for c in range(3)]
                rel = [state[3 + c : 4 + c] - sinks[3 + c] for c in range(3)]
                radius_sq = sep[0] * sep[0] + (sep[1] * sep[1] + (sep[2] * sep[2] + SOFTENING))
                radial = sep[0] * rel[0] + sep[1] * rel[1] + sep[2] * rel[2]
                inverse = lax.rsqrt(radius_sq)
                inverse_sq = inverse * inverse
                cube = inverse_sq * inverse
                fifth = (cube * inverse_sq) * radial
                load = 0 if step == 0 else None
                high, low = split2(cube)
                pltpu.matmul_acc_lhs(plain_acc[step], high, load_staged_rhs=load)
                pltpu.matmul_acc_lhs(plain_acc[step], low)
                high, low = split2(fifth)
                pltpu.matmul_acc_lhs(cross_acc[step], high, load_staged_rhs=load)
                pltpu.matmul_acc_lhs(cross_acc[step], low)

        def near_block(kind, number, n=0):
            if kind == "row":
                return row_block(number)
            return unit_block(*unit_place(number), n)

        near = [("row", n) for n in range(side)] + [("unit", 0, 0)]
        takes = {
            ("row", 0): [(take_row, 1), (take_row, 2)],
            ("row", 2): [(take_row, 3), (take_row, 4)],
            ("row", 4): [(take_row, 5), (take_row, 6)],
            ("row", 6): [(take_row, 7)],
            ("row", 7): [(take_unit, 0)],
        }
        for position, here in enumerate(near[:-1]):
            for take, number in takes.get(here, ()):
                take(number)
            pairs(near_block(*here), position & 1, near_block(*near[position + 1]))

        def one_unit(unit, last=False):
            part, w = unit_place(unit)
            for n in range(half):
                if n + 1 < half:
                    following = unit_block(part, w, n + 1)
                elif last:
                    following = None
                else:
                    take_unit(unit + 1)
                    following = unit_block(*unit_place(unit + 1), 0)
                pairs(unit_block(part, w, n), n & 1, following)

        def next_unit(unit, _):
            one_unit(unit)
            return 0

        lax.fori_loop(0, units - 1, next_unit, 0)
        one_unit(jnp.int32(units - 1), last=True)
        for core in range(cores):
            sums = [
                (pltpu.matmul_pop(plain_acc[t]) + pltpu.matmul_pop(cross_acc[t]))[:, :128]
                for t in range(core * half_tiles, (core + 1) * half_tiles)
            ]
            rows = jnp.transpose(jnp.concatenate(sums, axis=0))
            state = core_state(core)
            pos = state[0:3]
            vel = state[3:6]
            whole = rows[18:19] + rows[19:20] + rows[20:21]
            cross = rows[21:22] + rows[22:23] + rows[23:24]
            new_acc = (rows[0:3] + rows[3:6] + rows[6:9]) - pos * whole
            new_jerk = (rows[9:12] + rows[12:15] + rows[15:18]) - vel * whole + pos * cross
            part_ref[core] = jnp.concatenate(
                [new_acc, new_jerk, jnp.zeros((2, group), F32)], axis=0
            )

    pl.run_scoped(
        compute,
        *[pltpu.ACC(0)((tile, 256), F32) for _ in range(tiles)],
        *[pltpu.ACC(1)((tile, 256), F32) for _ in range(tiles)],
    )
    for step in peer_steps:
        part_copy(step).start()
    sum_ref[me] = part_ref[my_core]
    many(sum_ref, peers - 1, part_send, part_recv).wait_recv()

    total = sum_ref[0]
    for k in range(1, peers):
        total = total + sum_ref[k]
    total = jnp.where(lane_x == my_x, total, 0.0)
    rows = total[:, :slots]
    for x in range(1, xs):
        rows = rows + total[:, x * slots : (x + 1) * slots]
    own_rows = own_ref[...]
    is_live = lax.broadcasted_iota(jnp.int32, (1, slots), 1) < count_ref[...]
    out_ref[...] = correct(own_rows[0:6], own_rows[6:9], own_rows[9:12], rows, is_live)
    many(sink_ref, peers - 1, sink_send, sink_recv).wait_send()
    many(star_ref, side - 1, row_send, row_recv.at[0]).wait_send()
    many(star_ref, side * (side - 1), half_send, half_recv.at[0]).wait_send()
    many(sum_ref, peers - 1, part_send, part_recv).wait_send()


def solution(mesh):
    teams = mesh.shape["team"]
    cuts = mesh.shape["cuts"]
    xs = 4
    cores = 2
    blocks = teams * cuts // (xs * cores)

    def local(position, velocity, accel_old, jerk_old, star_mass, active_index, active_count):
        stars = position.shape[1]
        slots = active_index.shape[0]
        group = xs * slots
        vmem = pl.BlockSpec(memory_space=pltpu.VMEM)
        dma = pltpu.SemaphoreType.DMA
        return pl.pallas_call(
            functools.partial(step_kernel, teams, cuts, xs, slots, stars, cores),
            out_shape=jax.ShapeDtypeStruct((12, slots), F32),
            in_specs=[pl.BlockSpec(memory_space=pl.ANY)] * 7,
            out_specs=vmem,
            scratch_shapes=[
                *[pltpu.VMEM((3, stars), F32) for _ in range(4)],
                pltpu.VMEM((1, stars), F32),
                pltpu.VMEM((1, slots), jnp.int32),
                pltpu.VMEM((1, 1), jnp.int32),
                dma((7,)),
                pltpu.VMEM((16, slots), F32),
                pltpu.VMEM((blocks, 8, stars), F32),
                pltpu.VMEM((xs * cores, 8, group), F32),
                pltpu.VMEM((cores, 8, group), F32),
                pltpu.VMEM((xs * cores, 8, group), F32),
                pltpu.VMEM((2, 256, stars), BF16),
                pltpu.VMEM((2, 256, stars), BF16),
                pltpu.VMEM((6, cores * group, 128), F32),
                dma((teams // cores,)), dma((2 * (cuts // xs - 1),)), dma, dma, dma, dma, dma, dma,
            ],
            compiler_params=pltpu.CompilerParams(collective_id=0, has_side_effects=True),
            name="hermite_step",
        )(
            position, velocity, accel_old, jerk_old,
            star_mass.reshape(1, stars), active_index.reshape(1, slots), active_count.reshape(1, 1),
        )

    column = P(None, ("team", "cuts"))
    line = P(("team", "cuts"))
    return jax.shard_map(
        local, mesh=mesh, in_specs=(column, column, column, column, line, line, line),
        out_specs=column, check_vma=False,
    )
```
